512 devices in a mesh: grp: 16 (over z), dev: 32 (over y, x, core).
Axes of the slice: x: 4, y: 4, z: 16, core: 2. Of those that a mesh axis runs over, the one named last changes fastest.
Arguments:
- positions: float32 [3, 524288], P(None, ('grp', 'dev')), may hold values from -1 to 1
- forces: float32 [3, 524288], P(None, ('grp', 'dev')), may hold values from -4 to 4
- volumes: float32 [524288], P(('grp', 'dev')), may hold values from 0.02 to 0.2
- dest_bin: int32 [524288, 1], P(('grp', 'dev')), may hold values from 0 to 511; in each aligned block of 1024 rows (0 to 1023, 1024 to 2047, ...) at most 4 rows name the same one
- element: int32 [524288], P(('grp', 'dev')), may hold values from 0 to 127
Outputs:
- assembled: float32 [4, 216, 65536], P(None, None, ('grp', 'dev'))
The draws below stay inside these ranges and needn't reach their ends.
Inputs may be any that keep to these rules, and one draw needn't show every extreme that they name: `dest_bin`: no more than 4 of the particles of one device share a bin, and that number is reached.
All inputs are finite; a program needn't handle non-finite values.
Results may differ from the reference program's by a relative error of at most 0.0028.
Values sent between devices are 32-bit elements; how exact they have to be, the bound alone decides.
A program may use at most 64 MiB of HBM per device.

```python
import math
import jax
import jax.numpy as jnp
import numpy as np
from jax import lax

P_DEV = 1024
E_DEV = 128
CAP = 4
PARTICLES = 524288
N_GRP = 16
N_DEV = 32


def with_ends(drawn, stream_key, low, high):
    extent = drawn.shape
    spot = [jax.random.randint(jax.random.fold_in(stream_key, axis), (), 0, extent[axis]) for axis in range(len(extent))]
    drawn = drawn.at[tuple(spot)].set(low)
    longest = extent.index(max(extent))
    spot[longest] = (spot[longest] + 1) % extent[longest]
    return drawn.at[tuple(spot)].set(high)


def steps_of(key, extent, shards, smallest, high):
    gain, own = 1.0, jax.random.fold_in(key, 6)
    for dim, shards_of in shards:
        steps = jnp.exp(jax.random.uniform(jax.random.fold_in(own, dim), (shards_of,), jnp.float32, smallest / len(shards), high / len(shards)))
        gain = gain * jnp.repeat(steps, extent[dim] // shards_of).reshape([-1 if axis == dim else 1 for axis in range(len(extent))])
    return gain


def deal_out(stream_key, own, number, rows, number_of, top, reach, lean):
    sequence = jax.random.permutation(stream_key, number_of)
    crowded, usual = portions_of(number_of, rows * top, reach, lean, True), portions_of(number_of, rows * top, reach, lean, False)
    places = jnp.arange(number_of)

    def named(sizes, turn):
        used = int((sizes > 0).sum())
        fixed = max(1, used // 4)
        passed = fixed + (places - fixed + turn * (used - fixed)) % max(1, number_of - fixed)
        return jnp.zeros((number_of,), jnp.int32).at[sequence[jnp.where(places < fixed, places, passed)]].set(jnp.asarray(sizes, jnp.int32))

    sizes = jnp.where(number % 4 == 0, named(crowded, number // 4), named(usual, number - number // 4 - 1))
    mixed = jax.random.permutation(jax.random.fold_in(own, 3), number_of)
    source_of, sink = mixed[0:number_of // 2 * 2:2], mixed[1:number_of // 2 * 2:2]
    slack = jnp.minimum(sizes[source_of] - 1, reach - sizes[sink]) // 2
    slack = jnp.where((source_of == sequence[0]) | (sink == sequence[0]) | (sizes[sink] == 0), 0, jnp.maximum(slack, 0))
    passed = jax.random.randint(jax.random.fold_in(own, 4), (number_of // 2,), 0, 1 << 20) % (slack + 1)
    sizes = sizes.at[source_of].add(-passed).at[sink].add(passed)
    items = jnp.searchsorted(jnp.cumsum(sizes), jnp.arange(rows * top), side="right").astype(jnp.int32)
    table = items.reshape(top, rows).T
    table = table[jax.random.permutation(jax.random.fold_in(own, 1), rows)]
    turn = jax.random.randint(jax.random.fold_in(own, 2), (rows, 1), 0, top)
    return jnp.take_along_axis(table, (jnp.arange(top)[None, :] + turn) % top, axis=1)


def portions_of(amount, total, most, slope, full):
    loads = [(1 << 20) // math.isqrt(rank ** slope) + 1 for rank in range(1, amount + 1)]
    largest = most if full else min(most, max(-(-total // amount), total * loads[0] // sum(loads)))
    least = 1 if total - largest >= amount - 1 else 0
    counts, rest = [largest] + [least] * (amount - 1), total - largest - least * (amount - 1)
    while rest > 0:
        movable = [i for i in range(1, amount) if counts[i] < largest] or [i for i in range(1, amount) if counts[i] < most]
        mass, remaining = sum([loads[i] for i in movable]), rest
        for i in movable:
            addition = min(most - counts[i], max(1, remaining * loads[i] // mass), rest)
            counts[i] = counts[i] + addition
            rest = rest - addition
    return np.array(counts)


def centred(stream_key, extent, width, limit, cuts=(), held_as=jnp.bfloat16):
    factor_of = steps_of(stream_key, extent, cuts, -0.22, 0.18) if cuts else 1.0
    drawn = jax.random.normal(stream_key, extent, jnp.float32) * width * factor_of
    return jnp.minimum(jnp.maximum(drawn, -limit), limit).astype(held_as)


def setup_inputs(seed: int = 0) -> dict:
    seeds = jax.random.split(jax.random.key(seed), 6)
    positions = jnp.clip(jax.random.uniform(seeds[0], (3, PARTICLES), jnp.float32, -1.0, 1.0) * steps_of(seeds[0], (3, PARTICLES), ((1, 512),), -0.4, 0.0), -1.0, 1.0)
    forces = centred(seeds[1], (3, PARTICLES), 0.3, 4.0, ((1, 512),), jnp.float32)
    volumes = jnp.clip(jnp.exp(math.log(0.2) - 2.3025851 * jax.random.uniform(seeds[2], (PARTICLES,), jnp.float32) ** steps_of(seeds[2], (PARTICLES,), ((0, 512),), -0.2, 0.2)), 0.02, 0.2)
    dest_bin_keys = jax.random.split(jax.random.fold_in(seeds[3], 1), PARTICLES // P_DEV)
    dest_bin_turns = jax.random.permutation(jax.random.fold_in(seeds[3], 3), PARTICLES // P_DEV)
    dest_bin = jax.vmap(lambda own, number: deal_out(jax.random.fold_in(seeds[3], 2), own, number, P_DEV, N_GRP * N_DEV, 1, CAP, 2))(dest_bin_keys, dest_bin_turns).reshape((PARTICLES, 1))
    element = with_ends(jax.random.randint(seeds[4], (PARTICLES,), 0, E_DEV), jax.random.fold_in(seeds[4], 1), 0, E_DEV - 1).astype(jnp.int32)
    return dict(positions=positions, forces=forces, volumes=volumes, dest_bin=dest_bin, element=element)


gll_points = (-1.0, -0.765055323929465, -0.285231516480645, 0.285231516480645, 0.765055323929465, 1.0)


def tensor_weights(coords):
    nodes = jnp.array(gll_points, jnp.float32)
    w_r = jnp.exp(-((nodes[:, None] - coords[0][None, :]) ** 2) / 0.5)
    w_s = jnp.exp(-((nodes[:, None] - coords[1][None, :]) ** 2) / 0.5)
    w_t = jnp.exp(-((nodes[:, None] - coords[2][None, :]) ** 2) / 0.5)
    full = w_r[:, None, None, :] * w_s[None, :, None, :] * w_t[None, None, :, :]
    return full.reshape(216, coords.shape[1])


def reference(positions, forces, volumes, dest_bin, element):
    blocks = N_GRP * N_DEV
    total_elems = E_DEV * blocks
    glob = (dest_bin[:, 0] * E_DEV + element).astype(jnp.int32)
    pos_b = positions.reshape(3, blocks, P_DEV).transpose(1, 0, 2)
    frc_b = forces.reshape(3, blocks, P_DEV).transpose(1, 0, 2)
    vol_b = volumes.reshape(blocks, P_DEV)
    ids_b = glob.reshape(blocks, P_DEV)

    def step(acc, item):
        pos, frc, vol, ids = item
        weights = tensor_weights(pos)
        values = jnp.concatenate([vol[None, :], frc], 0)
        contrib = (values[:, None, :] * weights[None]).reshape(864, pos.shape[1])
        contrib = lax.optimization_barrier(contrib.astype(jnp.bfloat16)).astype(jnp.float32)
        acc = acc + jax.ops.segment_sum(contrib.T, ids, num_segments=total_elems)
        return acc, None

    acc0 = jnp.zeros((total_elems, 864), jnp.float32)
    acc, _ = lax.scan(step, acc0, (pos_b, frc_b, vol_b, ids_b))
    raw = acc.T.reshape(4, 6, 6, 6, total_elems)
    raw0 = raw[:, :, :, 0, :]
    raw5 = raw[:, :, :, 5, :]
    out = raw.at[:, :, :, 5, :-1].add(raw0[..., 1:])
    out = out.at[:, :, :, 0, 1:].add(raw5[..., :-1])
    return out.reshape(4, 216, total_elems)
```

```python
import functools

import jax
import jax.numpy as jnp
from jax import lax
from jax.experimental import pallas as pl
from jax.experimental.pallas import tpu as pltpu
from jax.sharding import PartitionSpec as P

MESH = pl.DeviceIdType.MESH
F32, BF16, I32 = jnp.float32, jnp.bfloat16, jnp.int32

GRP, DEV, SLOTS, LOCAL, ELEMS = 16, 32, 4, 1024, 128
TILE = 128
NEAR = 4

gll_points = (
    -1.0,
    -0.765055323929465,
    -0.285231516480645,
    0.285231516480645,
    0.765055323929465,
    1.0,
)


def iota(shape, axis):
    return lax.broadcasted_iota(I32, shape, axis)


def roll(x, shift, axis):
    shift = shift % x.shape[axis]
    return x if shift == 0 else pltpu.roll(x, shift, axis)


def dot_nt(a, b):
    return lax.dot_general(a, b, (((1,), (1,)), ((), ())), preferred_element_type=F32)


def rank_in_bin(target):
    blocks = LOCAL // TILE
    row = target.astype(F32)
    parts = [row[:, b * TILE:(b + 1) * TILE] for b in range(blocks)]
    columns = [jnp.transpose(jnp.broadcast_to(part, (TILE, TILE))) for part in parts]
    earlier = iota((TILE, TILE), 0) < iota((TILE, TILE), 1)
    ranks = []
    for p in range(blocks):
        own = (columns[p] == parts[p]) & earlier
        total = jnp.where(own, 1.0, 0.0)
        for q in range(p):
            total = total + jnp.where(columns[q] == parts[p], 1.0, 0.0)
        ranks.append(jnp.sum(total, axis=0, keepdims=True))
    return jnp.concatenate(ranks, axis=1).astype(I32)


def pieces(x):
    high = x.astype(BF16).astype(F32)
    rest = x - high
    mid = rest.astype(BF16).astype(F32)
    return high, mid, rest - mid


def pack(positions, forces, volumes, target, element):
    code = (target // DEV) * SLOTS + rank_in_bin(target)
    lane_of = iota((TILE, LOCAL), 0)
    mine = (lane_of // 4) == target % DEV
    sub = iota((8, LOCAL), 0) % 4
    rows = (
        (positions[0:1], positions[1:2], positions[2:3], element.astype(F32)),
        (forces[0:1], forces[1:2], forces[2:3], volumes),
    )
    out = None
    for half, (f0, f1, f2, f3) in enumerate(rows):
        feats = jnp.where(sub == 0, f0, jnp.where(sub == 1, f1, jnp.where(sub == 2, f2, f3)))
        left = jnp.concatenate(
            [
                jnp.where(mine, jnp.concatenate([piece] * 16, axis=0), 0.0).astype(BF16)
                for piece in pieces(feats)
            ],
            axis=0,
        )
        right = jnp.where(lane_of == code + half * 64, 1.0, 0.0).astype(BF16)
        prod = dot_nt(left, right)
        part = prod[0:128] + prod[128:256] + prod[256:384]
        out = part if out is None else out + part
    return out


def to_group_tiles(tiles):
    sub, lane = iota((8, TILE), 0), iota((8, TILE), 1)
    keep = (sub // 4) == (lane // 64)
    tiles = [jnp.where(keep, x, roll(roll(x, 4, 0), 64, 1)) for x in tiles]
    for bit in range(4):
        step = 4 << bit
        low = (lane // step) % 2 == 0
        new = list(tiles)
        for v in range(16):
            if not (v >> bit) & 1:
                a, b = tiles[v], tiles[v | (1 << bit)]
                new[v] = jnp.where(low, a, roll(b, step, 1))
                new[v | (1 << bit)] = jnp.where(low, roll(a, -step, 1), b)
        tiles = new
    return tiles


def by_row(sub, labels, parts):
    out = parts[labels[0]]
    for s in range(1, 8):
        if labels[s] != labels[s - 1]:
            out = jnp.where(sub >= s, parts[labels[s]], out)
    return out


def weigh(x):
    width = x.shape[1]
    shape = (8, width)
    sub = iota(shape, 0)
    nodes = jnp.full(shape, gll_points[5], F32)
    for n in range(5):
        nodes = jnp.where(sub == n, gll_points[n], nodes)
    w_r, w_s, w_t = [jnp.exp(-((nodes - x[d:d + 1]) ** 2) / 0.5) for d in range(3)]
    r_rows = [jnp.broadcast_to(w_r[i:i + 1], shape) for i in range(6)]
    s_cycle = (
        jnp.where(sub < 6, w_s, roll(w_s, 6, 0)),
        jnp.where(sub < 4, roll(w_s, 6, 0), roll(w_s, 4, 0)),
        jnp.where(sub < 2, roll(w_s, 4, 0), roll(w_s, 2, 0)),
    )
    faces = [
        by_row(sub, [((8 * b + s) % 36) // 6 for s in range(8)], r_rows) * s_cycle[b % 3]
        for b in range(9)
    ]
    values = [jnp.broadcast_to(x[d:d + 1], shape) for d in (7, 4, 5, 6)]
    scaled = [
        by_row(sub, [(8 * b + s) // 36 for s in range(8)], values) * faces[b % 9]
        for b in range(18)
    ]
    onehot = jnp.where(iota((ELEMS, width), 0) == x[3:4].astype(I32), 1.0, 0.0).astype(BF16)
    return scaled, w_t, onehot


def slab(scaled, w_t, onehot, k):
    weight = jnp.broadcast_to(w_t[k:k + 1], scaled[0].shape)
    contrib = jnp.concatenate([part * weight for part in scaled], axis=0).astype(BF16)
    return dot_nt(contrib, onehot)


def kernel(
    pos_ref, frc_ref, vol_ref, bin_ref, elem_ref, out_ref,
    send1, recv1, send2, recv2, acc, rim_out, rim_in,
    send1_sem, recv1_sem, send2_sem, recv2_sem, near_sem, rim_send_sem, rim_recv_sem,
):
    g, d = lax.axis_index("grp"), lax.axis_index("dev")
    y, x, core = d // 8, (d // 2) % 4, d % 2

    def far_first(items):
        return sorted(items, key=lambda m: -(min(m[0], 4 - m[0]) + min(m[1], 4 - m[1])))

    moves = far_first(
        [(dy, dx, dc) for dy in range(4) for dx in range(4) for dc in range(2) if dy or dx or dc]
    )
    peers = [
        (lax.rem(y + dy, 4) * 4 + lax.rem(x + dx, 4)) * 2 + lax.rem(core + dc, 2)
        for dy, dx, dc in moves
    ]

    barrier = pltpu.get_barrier_semaphore()
    for step in [s for n in range(NEAR, 0, -1) for s in (n, GRP - n)]:
        pl.semaphore_signal(
            barrier, 1, device_id={"grp": lax.rem(g + step, GRP), "dev": d}, device_id_type=MESH
        )
    for peer in peers:
        pl.semaphore_signal(barrier, 1, device_id={"grp": g, "dev": peer}, device_id_type=MESH)

    packed = pack(pos_ref[...], frc_ref[...], vol_ref[...], bin_ref[...], elem_ref[...])
    send1[...] = packed.reshape(send1.shape)
    acc[...] = jnp.zeros_like(acc)
    recv1[d] = send1[d]

    pl.semaphore_wait(barrier, 2 * NEAR + DEV - 1)
    for step in (NEAR, GRP - NEAR):
        pl.semaphore_signal(
            near_sem, 1, device_id={"grp": lax.rem(g + step, GRP), "dev": d}, device_id_type=MESH
        )
    for peer in peers:
        pltpu.make_async_remote_copy(
            src_ref=send1.at[peer],
            dst_ref=recv1.at[d],
            send_sem=send1_sem,
            recv_sem=recv1_sem,
            device_id={"grp": g, "dev": peer},
            device_id_type=MESH,
        ).start()
    others = recv1.at[pl.ds(0, DEV - 1)]
    pltpu.make_async_copy(others, others, recv1_sem).wait()

    arrived = recv1[...].reshape(16, 8, TILE)
    tiles = to_group_tiles([arrived[v] for v in range(16)])
    for v in range(16):
        send2[v] = tiles[v]
    recv2[g] = send2[g]

    pl.semaphore_wait(near_sem, 2)
    for step in [8] + [s for n in range(7, 0, -1) for s in (n, GRP - n)]:
        to = lax.rem(g + step, GRP)
        pltpu.make_async_remote_copy(
            src_ref=send2.at[to],
            dst_ref=recv2.at[g],
            send_sem=send2_sem,
            recv_sem=recv2_sem.at[step],
            device_id={"grp": to, "dev": d},
            device_id_type=MESH,
        ).start()

    def await_step(step):
        source = lax.rem(g - step + GRP, GRP)
        pltpu.make_async_copy(recv2.at[source], recv2.at[source], recv2_sem.at[step]).wait()
        return recv2[source]

    def body(n, carry):
        pair = jnp.concatenate([await_step(n), await_step(GRP - n)], axis=1)
        scaled, w_t, onehot = weigh(pair)
        for k in range(6):
            acc[k] += slab(scaled, w_t, onehot, k)
        return carry

    lax.fori_loop(1, 8, body, 0)

    pair = jnp.concatenate([recv2[g], await_step(8)], axis=1)
    scaled, w_t, onehot = weigh(pair)
    sub, lane = iota((8, TILE), 0), iota((8, TILE), 1)
    raw0 = acc[0] + slab(scaled, w_t, onehot, 0)
    raw5 = acc[5] + slab(scaled, w_t, onehot, 5)
    to_prev, to_next = jnp.zeros((8, TILE), F32), jnp.zeros((8, TILE), F32)
    for b in range(18):
        to_prev = jnp.where(lane == b, roll(raw0[8 * b:8 * b + 8], b, 1), to_prev)
        to_next = jnp.where(lane == b, roll(raw5[8 * b:8 * b + 8], b + 1, 1), to_next)
    rim_out[0] = to_prev
    rim_out[1] = to_next
    me = g * DEV + d
    ends = []
    for way, step in ((0, GRP * DEV - 1), (1, 1)):
        to = lax.rem(me + step, GRP * DEV)
        end = pltpu.make_async_remote_copy(
            src_ref=rim_out.at[way],
            dst_ref=rim_in.at[way],
            send_sem=rim_send_sem.at[way],
            recv_sem=rim_recv_sem.at[way],
            device_id={"grp": to // DEV, "dev": lax.rem(to, DEV)},
            device_id_type=MESH,
        )
        end.start()
        ends.append(end)

    for k in range(1, 5):
        out_ref[pl.ds(k, 144, stride=6), :] = acc[k] + slab(scaled, w_t, onehot, k)

    for end in ends:
        end.wait()
    from_next = jnp.where(me == GRP * DEV - 1, 0.0, rim_in[0])
    from_prev = jnp.where(me == 0, 0.0, rim_in[1])
    out5, out0 = [], []
    for b in range(18):
        block0, block5 = raw0[8 * b:8 * b + 8], raw5[8 * b:8 * b + 8]
        after = jnp.where(lane == TILE - 1, roll(from_next, TILE - 1 - b, 1), roll(block0, -1, 1))
        before = jnp.where(lane == 0, roll(from_prev, -b, 1), roll(block5, 1, 1))
        out5.append(block5 + after)
        out0.append(block0 + before)
    out_ref[pl.ds(0, 144, stride=6), :] = jnp.concatenate(out0, axis=0)
    out_ref[pl.ds(5, 144, stride=6), :] = jnp.concatenate(out5, axis=0)

    sent1 = send1.at[pl.ds(0, DEV - 1)]
    pltpu.make_async_copy(sent1, sent1, send1_sem).wait()
    sent2 = send2.at[pl.ds(0, GRP - 1)]
    pltpu.make_async_copy(sent2, sent2, send2_sem).wait()


def per_device(positions, forces, volumes, dest_bin, element):
    vmem = pl.BlockSpec(memory_space=pltpu.VMEM)
    dma = pltpu.SemaphoreType.DMA
    out = pl.pallas_call(
        kernel,
        out_shape=jax.ShapeDtypeStruct((864, ELEMS), F32),
        in_specs=[vmem] * 5,
        out_specs=vmem,
        scratch_shapes=[
            pltpu.VMEM((DEV, 4, TILE), F32),
            pltpu.VMEM((DEV, 4, TILE), F32),
            pltpu.VMEM((GRP, 8, TILE), F32),
            pltpu.VMEM((GRP, 8, TILE), F32),
            pltpu.VMEM((6, 144, ELEMS), F32),
            pltpu.VMEM((2, 8, TILE), F32),
            pltpu.VMEM((2, 8, TILE), F32),
            dma, dma, dma, dma((GRP,)), pltpu.SemaphoreType.REGULAR, dma((2,)), dma((2,)),
        ],
        compiler_params=pltpu.CompilerParams(collective_id=0, has_side_effects=True),
        name="project",
    )(
        positions,
        forces,
        volumes.reshape(1, LOCAL),
        dest_bin.reshape(1, LOCAL),
        element.reshape(1, LOCAL),
    )
    return out.reshape(4, 216, ELEMS)


def solution(mesh):
    in_specs = (
        P(None, ("grp", "dev")),
        P(None, ("grp", "dev")),
        P(("grp", "dev")),
        P(("grp", "dev"), None),
        P(("grp", "dev")),
    )
    out_specs = P(None, None, ("grp", "dev"))
    return jax.shard_map(
        per_device, mesh=mesh, in_specs=in_specs, out_specs=out_specs, check_vma=False
    )
```

```python
import functools

import jax
import jax.numpy as jnp
from jax import lax
from jax.experimental import pallas as pl
from jax.experimental.pallas import tpu as pltpu
from jax.sharding import PartitionSpec as P

MESH = pl.DeviceIdType.MESH
F32, BF16, I32 = jnp.float32, jnp.bfloat16, jnp.int32

GRP, DEV, SLOTS, LOCAL, ELEMS = 16, 32, 4, 1024, 128
TILE = 128
HALF = 8

gll_points = (
    -1.0,
    -0.765055323929465,
    -0.285231516480645,
    0.285231516480645,
    0.765055323929465,
    1.0,
)


def iota(shape, axis):
    return lax.broadcasted_iota(I32, shape, axis)


def roll(x, shift, axis):
    shift = shift % x.shape[axis]
    return x if shift == 0 else pltpu.roll(x, shift, axis)


def dot_nt(a, b):
    return lax.dot_general(a, b, (((1,), (1,)), ((), ())), preferred_element_type=F32)


def rank_in_bin(target):
    blocks = LOCAL // TILE
    row = target.astype(F32)
    parts = [row[:, b * TILE:(b + 1) * TILE] for b in range(blocks)]
    columns = [jnp.transpose(jnp.broadcast_to(part, (TILE, TILE))) for part in parts]
    earlier = iota((TILE, TILE), 0) < iota((TILE, TILE), 1)
    ranks = []
    for p in range(blocks):
        own = (columns[p] == parts[p]) & earlier
        total = jnp.where(own, 1.0, 0.0)
        for q in range(p):
            total = total + jnp.where(columns[q] == parts[p], 1.0, 0.0)
        ranks.append(jnp.sum(total, axis=0, keepdims=True))
    return jnp.concatenate(ranks, axis=1).astype(I32)


def pieces(x):
    high = x.astype(BF16).astype(F32)
    rest = x - high
    mid = rest.astype(BF16).astype(F32)
    return high, mid, rest - mid


def pack(positions, forces, volumes, target, element):
    dev = target % DEV
    code = (dev % 2) * 64 + (dev // 2) * SLOTS + rank_in_bin(target)
    row_of = iota((TILE, LOCAL), 0)
    mine = (row_of // 8) == target // DEV
    sub = iota((8, LOCAL), 0)
    parts = [positions[n:n + 1] for n in range(3)] + [element.astype(F32)]
    parts += [forces[n:n + 1] for n in range(3)] + [volumes]
    feats = parts[7]
    for n in range(7):
        feats = jnp.where(sub == n, parts[n], feats)
    left = jnp.concatenate(
        [
            jnp.where(mine, jnp.concatenate([piece] * 16, axis=0), 0.0).astype(BF16)
            for piece in pieces(feats)
        ],
        axis=0,
    )
    right = jnp.where(row_of == code, 1.0, 0.0).astype(BF16)
    prod = dot_nt(left, right)
    return prod[0:128] + prod[128:256] + prod[256:384]


def swap_halves(x):
    sub, lane = iota((8, TILE), 0), iota((8, TILE), 1)
    return jnp.where((sub // 4) == (lane // 64), x, roll(roll(x, 4, 0), 64, 1))


def to_dev_tiles(tiles):
    lane = iota((8, TILE), 1)
    for bit in range(4):
        step = 4 << bit
        low = (lane // step) % 2 == 0
        new = list(tiles)
        for v in range(16):
            if not (v >> bit) & 1:
                a, b = tiles[v], tiles[v | (1 << bit)]
                new[v] = jnp.where(low, a, roll(b, step, 1))
                new[v | (1 << bit)] = jnp.where(low, roll(a, -step, 1), b)
        tiles = new
    return [swap_halves(x) for x in tiles]


def by_row(sub, labels, parts):
    out = parts[labels[0]]
    for s in range(1, 8):
        if labels[s] != labels[s - 1]:
            out = jnp.where(sub >= s, parts[labels[s]], out)
    return out


def weigh(x):
    width = x.shape[1]
    shape = (8, width)
    sub = iota(shape, 0)
    nodes = jnp.full(shape, gll_points[5], F32)
    for n in range(5):
        nodes = jnp.where(sub == n, gll_points[n], nodes)
    w_r, w_s, w_t = [jnp.exp(-((nodes - x[d:d + 1]) ** 2) / 0.5) for d in range(3)]
    r_rows = [jnp.broadcast_to(w_r[i:i + 1], shape) for i in range(6)]
    s_cycle = (
        jnp.where(sub < 6, w_s, roll(w_s, 6, 0)),
        jnp.where(sub < 4, roll(w_s, 6, 0), roll(w_s, 4, 0)),
        jnp.where(sub < 2, roll(w_s, 4, 0), roll(w_s, 2, 0)),
    )
    faces = [
        by_row(sub, [((8 * b + s) % 36) // 6 for s in range(8)], r_rows) * s_cycle[b % 3]
        for b in range(9)
    ]
    values = [jnp.broadcast_to(x[d:d + 1], shape) for d in (7, 4, 5, 6)]
    scaled = [
        by_row(sub, [(8 * b + s) // 36 for s in range(8)], values) * faces[b % 9]
        for b in range(18)
    ]
    onehot = jnp.where(iota((ELEMS, width), 0) == x[3:4].astype(I32), 1.0, 0.0).astype(BF16)
    return scaled, w_t, onehot


def slab(scaled, w_t, onehot, k):
    weight = jnp.broadcast_to(w_t[k:k + 1], scaled[0].shape)
    contrib = jnp.concatenate([part * weight for part in scaled], axis=0).astype(BF16)
    return dot_nt(contrib, onehot)


CHIPS = sorted(
    [(dy, dx) for dy in range(4) for dx in range(4)],
    key=lambda m: min(m[0], 4 - m[0]) + min(m[1], 4 - m[1]),
)


def table(values):
    return sum(v << (2 * n) for n, v in enumerate(values))


def kernel(
    pos_hbm, frc_hbm, vol_hbm, bin_hbm, elem_hbm, out_ref,
    pos_ref, frc_ref, vol_ref, bin_ref, elem_ref,
    send1, recv1, send2, recv2, acc, rim_out, rim_in,
    in_sem, send1_sem, recv1_sem, send2_sem, recv2_sem, late_sem, all_sem, dev_sem,
    rim_send_sem, rim_recv_sem,
):
    g, d = lax.axis_index("grp"), lax.axis_index("dev")
    y, x, core = d // 8, (d // 2) % 4, d % 2
    late = g // HALF

    loads = []
    for n, (src, dst) in enumerate((
        (bin_hbm, bin_ref), (pos_hbm, pos_ref), (frc_hbm, frc_ref),
        (vol_hbm, vol_ref), (elem_hbm, elem_ref),
    )):
        load = pltpu.make_async_copy(src, dst, in_sem.at[n])
        load.start()
        loads.append(load)

    def device(dy, dx, dc):
        return (lax.rem(y + dy, 4) * 4 + lax.rem(x + dx, 4)) * 2 + lax.rem(core + dc, 2)

    def greet(sem, grp, dev):
        pl.semaphore_signal(sem, 1, device_id={"grp": grp, "dev": dev}, device_id_type=MESH)

    barrier = pltpu.get_barrier_semaphore()
    row = [(0, dx, dc) for dx in (2, 1, 3, 0) for dc in range(2) if dx or dc]
    column = [(dy, 0, 0) for dy in (2, 1, 3)]
    for move in row + column:
        greet(barrier, g, device(*move))

    @pl.when(late == 0)
    def _():
        for step in [8] + [s for n in range(7, 0, -1) for s in (n, GRP - n)]:
            greet(barrier, lax.rem(g + step, GRP), d)

    for load in loads:
        load.wait()
    packed = pack(pos_ref[...], frc_ref[...], vol_ref[...], bin_ref[...], elem_ref[...])
    send1[...] = packed.reshape(send1.shape)

    pl.semaphore_wait(barrier, len(row) + len(column) + HALF - 1 + late)

    def send_grp(to):
        pltpu.make_async_remote_copy(
            src_ref=send1.at[to],
            dst_ref=recv1.at[g],
            send_sem=send1_sem,
            recv_sem=recv1_sem,
            device_id={"grp": to, "dev": d},
            device_id_type=MESH,
        ).start()

    def send_own_half():
        for step in range(1, HALF):
            send_grp(late * HALF + lax.rem(g + step, HALF))

    def send_other_half():
        for n in range(HALF):
            send_grp((1 - late) * HALF + n)

    @pl.when(late == 0)
    def _():
        send_own_half()

    @pl.when(late == 1)
    def _():
        send_other_half()
        for n in range(HALF):
            greet(late_sem, n, d)

    for move in column:
        greet(dev_sem, g, device(*move))
    acc[...] = jnp.zeros_like(acc)
    recv1[g] = send1[g]

    @pl.when(late == 0)
    def _():
        pl.semaphore_wait(late_sem, HALF)

        @pl.when(g == 0)
        def _():
            for n in range(HALF // 2):
                greet(all_sem, GRP - 1 - n, d)

        @pl.when(g == HALF - 1)
        def _():
            for n in range(HALF // 2):
                greet(all_sem, HALF + n, d)

        send_other_half()

    @pl.when(late == 1)
    def _():
        pl.semaphore_wait(all_sem, 1)
        send_own_half()

    pl.semaphore_wait(dev_sem, len(column))
    others = recv1.at[pl.ds(0, GRP - 1)]
    pltpu.make_async_copy(others, others, recv1_sem).wait()

    tiles = to_dev_tiles([recv1[v] for v in range(16)])
    send2[...] = jnp.concatenate(tiles, axis=0).reshape(send2.shape)
    for n in range(15, -1, -1):
        dy, dx = CHIPS[n]
        for dc in range(2):
            if n or dc:
                peer = device((4 - dy) % 4, (4 - dx) % 4, dc)
                pltpu.make_async_remote_copy(
                    src_ref=send2.at[peer],
                    dst_ref=recv2.at[d],
                    send_sem=send2_sem,
                    recv_sem=recv2_sem.at[n // 2],
                    device_id={"grp": g, "dev": peer},
                    device_id_type=MESH,
                ).start()
    recv2[d] = send2[d]

    def chip_tile(n, of):
        shift = 2 * n
        dy = (table([m[0] for m in CHIPS[of::2]]) >> shift) % 4
        dx = (table([m[1] for m in CHIPS[of::2]]) >> shift) % 4
        first = (lax.rem(y + dy, 4) * 4 + lax.rem(x + dx, 4)) * 2
        return swap_halves(recv2[pl.ds(first, 2)].reshape(8, TILE))

    def chunk(n, count):
        part = recv2.at[pl.ds(0, count)]
        pltpu.make_async_copy(part, part, recv2_sem.at[n]).wait()
        return jnp.concatenate([chip_tile(n, 0), chip_tile(n, 1)], axis=1)

    def add_chunk(pair):
        scaled, w_t, onehot = weigh(pair)
        for k in range(6):
            acc[k] += slab(scaled, w_t, onehot, k)

    def body(n, carry):
        @pl.when(n == 0)
        def _():
            part = recv2.at[pl.ds(0, 3)]
            pltpu.make_async_copy(part, part, recv2_sem.at[n]).wait()

        @pl.when(n > 0)
        def _():
            part = recv2.at[pl.ds(0, 4)]
            pltpu.make_async_copy(part, part, recv2_sem.at[n]).wait()

        add_chunk(jnp.concatenate([chip_tile(n, 0), chip_tile(n, 1)], axis=1))
        return carry

    lax.fori_loop(0, 7, body, 0)

    pair = chunk(7, 4)
    scaled, w_t, onehot = weigh(pair)
    sub, lane = iota((8, TILE), 0), iota((8, TILE), 1)
    raw0 = acc[0] + slab(scaled, w_t, onehot, 0)
    raw5 = acc[5] + slab(scaled, w_t, onehot, 5)
    to_prev, to_next = jnp.zeros((8, TILE), F32), jnp.zeros((8, TILE), F32)
    for b in range(18):
        to_prev = jnp.where(lane == b, roll(raw0[8 * b:8 * b + 8], b, 1), to_prev)
        to_next = jnp.where(lane == b, roll(raw5[8 * b:8 * b + 8], b + 1, 1), to_next)
    rim_out[0] = to_prev
    rim_out[1] = to_next
    me = g * DEV + d
    ends = []
    for way, step in ((0, GRP * DEV - 1), (1, 1)):
        to = lax.rem(me + step, GRP * DEV)
        end = pltpu.make_async_remote_copy(
            src_ref=rim_out.at[way],
            dst_ref=rim_in.at[way],
            send_sem=rim_send_sem.at[way],
            recv_sem=rim_recv_sem.at[way],
            device_id={"grp": to // DEV, "dev": lax.rem(to, DEV)},
            device_id_type=MESH,
        )
        end.start()
        ends.append(end)

    for k in range(1, 5):
        out_ref[pl.ds(k, 144, stride=6), :] = acc[k] + slab(scaled, w_t, onehot, k)

    for end in ends:
        end.wait()
    from_next = jnp.where(me == GRP * DEV - 1, 0.0, rim_in[0])
    from_prev = jnp.where(me == 0, 0.0, rim_in[1])
    out5, out0 = [], []
    for b in range(18):
        block0, block5 = raw0[8 * b:8 * b + 8], raw5[8 * b:8 * b + 8]
        after = jnp.where(lane == TILE - 1, roll(from_next, TILE - 1 - b, 1), roll(block0, -1, 1))
        before = jnp.where(lane == 0, roll(from_prev, -b, 1), roll(block5, 1, 1))
        out5.append(block5 + after)
        out0.append(block0 + before)
    out_ref[pl.ds(0, 144, stride=6), :] = jnp.concatenate(out0, axis=0)
    out_ref[pl.ds(5, 144, stride=6), :] = jnp.concatenate(out5, axis=0)

    sent1 = send1.at[pl.ds(0, GRP - 1)]
    pltpu.make_async_copy(sent1, sent1, send1_sem).wait()
    sent2 = send2.at[pl.ds(0, DEV - 1)]
    pltpu.make_async_copy(sent2, sent2, send2_sem).wait()


def per_device(positions, forces, volumes, dest_bin, element):
    vmem = pl.BlockSpec(memory_space=pltpu.VMEM)
    dma, regular = pltpu.SemaphoreType.DMA, pltpu.SemaphoreType.REGULAR
    out = pl.pallas_call(
        kernel,
        out_shape=jax.ShapeDtypeStruct((864, ELEMS), F32),
        in_specs=[pl.BlockSpec(memory_space=pl.ANY)] * 5,
        out_specs=vmem,
        scratch_shapes=[
            pltpu.VMEM((3, LOCAL), F32),
            pltpu.VMEM((3, LOCAL), F32),
            pltpu.VMEM((1, LOCAL), F32),
            pltpu.VMEM((1, LOCAL), I32),
            pltpu.VMEM((1, LOCAL), I32),
            pltpu.VMEM((GRP, 8, TILE), F32),
            pltpu.VMEM((GRP, 8, TILE), F32),
            pltpu.VMEM((DEV, 4, TILE), F32),
            pltpu.VMEM((DEV, 4, TILE), F32),
            pltpu.VMEM((6, 144, ELEMS), F32),
            pltpu.VMEM((2, 8, TILE), F32),
            pltpu.VMEM((2, 8, TILE), F32),
            dma((5,)), dma, dma, dma, dma((8,)), regular, regular, regular,
            dma((2,)), dma((2,)),
        ],
        compiler_params=pltpu.CompilerParams(collective_id=0, has_side_effects=True),
        name="project",
    )(
        positions,
        forces,
        volumes.reshape(1, LOCAL),
        dest_bin.reshape(1, LOCAL),
        element.reshape(1, LOCAL),
    )
    return out.reshape(4, 216, ELEMS)


def solution(mesh):
    in_specs = (
        P(None, ("grp", "dev")),
        P(None, ("grp", "dev")),
        P(("grp", "dev")),
        P(("grp", "dev"), None),
        P(("grp", "dev")),
    )
    out_specs = P(None, None, ("grp", "dev"))
    return jax.shard_map(
        per_device, mesh=mesh, in_specs=in_specs, out_specs=out_specs, check_vma=False
    )
```

```python
import functools

import jax
import jax.numpy as jnp
from jax import lax
from jax.experimental import pallas as pl
from jax.experimental.pallas import tpu as pltpu
from jax.sharding import PartitionSpec as P

MESH = pl.DeviceIdType.MESH
F32, BF16, I32 = jnp.float32, jnp.bfloat16, jnp.int32

GRP, DEV, SLOTS, LOCAL, ELEMS = 16, 32, 4, 1024, 128
TILE = 128
HALF = 8

gll_points = (
    -1.0,
    -0.765055323929465,
    -0.285231516480645,
    0.285231516480645,
    0.765055323929465,
    1.0,
)


def iota(shape, axis):
    return lax.broadcasted_iota(I32, shape, axis)


def roll(x, shift, axis):
    shift = shift % x.shape[axis]
    return x if shift == 0 else pltpu.roll(x, shift, axis)


def dot_nt(a, b):
    return lax.dot_general(a, b, (((1,), (1,)), ((), ())), preferred_element_type=F32)


def rank_in_bin(target):
    blocks = LOCAL // TILE
    row = target.astype(F32)
    parts = [row[:, b * TILE:(b + 1) * TILE] for b in range(blocks)]
    columns = [jnp.transpose(jnp.broadcast_to(part, (TILE, TILE))) for part in parts]
    earlier = iota((TILE, TILE), 0) < iota((TILE, TILE), 1)
    ranks = []
    for p in range(blocks):
        own = (columns[p] == parts[p]) & earlier
        total = jnp.where(own, 1.0, 0.0)
        for q in range(p):
            total = total + jnp.where(columns[q] == parts[p], 1.0, 0.0)
        ranks.append(jnp.sum(total, axis=0, keepdims=True))
    return jnp.concatenate(ranks, axis=1).astype(I32)


def pieces(x):
    high = x.astype(BF16).astype(F32)
    rest = x - high
    mid = rest.astype(BF16).astype(F32)
    return high, mid, rest - mid


def pack(positions, forces, volumes, target, element):
    dev = target % DEV
    code = (dev % 2) * 64 + (dev // 2) * SLOTS + rank_in_bin(target)
    row_of = iota((TILE, LOCAL), 0)
    mine = (row_of // 8) == target // DEV
    sub = iota((8, LOCAL), 0)
    parts = [positions[n:n + 1] for n in range(3)] + [element.astype(F32)]
    parts += [forces[n:n + 1] for n in range(3)] + [volumes]
    feats = parts[7]
    for n in range(7):
        feats = jnp.where(sub == n, parts[n], feats)
    left = jnp.concatenate(
        [
            jnp.where(mine, jnp.concatenate([piece] * 16, axis=0), 0.0).astype(BF16)
            for piece in pieces(feats)
        ],
        axis=0,
    )
    right = jnp.where(row_of == code, 1.0, 0.0).astype(BF16)
    prod = dot_nt(left, right)
    return prod[0:128] + prod[128:256] + prod[256:384]


def swap_halves(x):
    sub, lane = iota((8, TILE), 0), iota((8, TILE), 1)
    return jnp.where((sub // 4) == (lane // 64), x, roll(roll(x, 4, 0), 64, 1))


def to_dev_tiles(tiles):
    lane = iota((8, TILE), 1)
    for bit in range(4):
        step = 4 << bit
        low = (lane // step) % 2 == 0
        new = list(tiles)
        for v in range(16):
            if not (v >> bit) & 1:
                a, b = tiles[v], tiles[v | (1 << bit)]
                new[v] = jnp.where(low, a, roll(b, step, 1))
                new[v | (1 << bit)] = jnp.where(low, roll(a, -step, 1), b)
        tiles = new
    return [swap_halves(x) for x in tiles]


def by_row(sub, labels, parts):
    out = parts[labels[0]]
    for s in range(1, 8):
        if labels[s] != labels[s - 1]:
            out = jnp.where(sub >= s, parts[labels[s]], out)
    return out


def weigh(x):
    width = x.shape[1]
    shape = (8, width)
    sub = iota(shape, 0)
    nodes = jnp.full(shape, gll_points[5], F32)
    for n in range(5):
        nodes = jnp.where(sub == n, gll_points[n], nodes)
    w_r, w_s, w_t = [jnp.exp(-((nodes - x[d:d + 1]) ** 2) / 0.5) for d in range(3)]
    r_rows = [jnp.broadcast_to(w_r[i:i + 1], shape) for i in range(6)]
    s_cycle = (
        jnp.where(sub < 6, w_s, roll(w_s, 6, 0)),
        jnp.where(sub < 4, roll(w_s, 6, 0), roll(w_s, 4, 0)),
        jnp.where(sub < 2, roll(w_s, 4, 0), roll(w_s, 2, 0)),
    )
    faces = [
        by_row(sub, [((8 * b + s) % 36) // 6 for s in range(8)], r_rows) * s_cycle[b % 3]
        for b in range(9)
    ]
    values = [jnp.broadcast_to(x[d:d + 1], shape) for d in (7, 4, 5, 6)]
    scaled = [
        by_row(sub, [(8 * b + s) // 36 for s in range(8)], values) * faces[b % 9]
        for b in range(18)
    ]
    onehot = jnp.where(iota((ELEMS, width), 0) == x[3:4].astype(I32), 1.0, 0.0).astype(BF16)
    return scaled, w_t, onehot


def slabs(x):
    scaled, w_t, onehot = weigh(x)
    rows = []
    for k in range(6):
        weight = jnp.broadcast_to(w_t[k:k + 1], scaled[0].shape)
        rows += [part * weight for part in scaled]
    return dot_nt(jnp.concatenate(rows, axis=0).astype(BF16), onehot)


CHIPS = sorted(
    [(dy, dx) for dy in range(4) for dx in range(4)],
    key=lambda m: min(m[0], 4 - m[0]) + min(m[1], 4 - m[1]),
)


def kernel(
    pos_hbm, frc_hbm, vol_hbm, bin_hbm, elem_hbm, out_ref,
    pos_ref, frc_ref, vol_ref, bin_ref, elem_ref,
    send1, recv1, send2, recv2, acc, rim_out, rim_in,
    in_sem, send1_sem, recv1_sem, send2_sem, recv2_sem, late_sem, near_sem, far_sem, dev_sem,
    rim_send_sem, rim_recv_sem,
):
    g, d = lax.axis_index("grp"), lax.axis_index("dev")
    y, x, core = d // 8, (d // 2) % 4, d % 2
    late = g // HALF

    loads = []
    for n, (src, dst) in enumerate((
        (bin_hbm, bin_ref), (pos_hbm, pos_ref), (frc_hbm, frc_ref),
        (vol_hbm, vol_ref), (elem_hbm, elem_ref),
    )):
        load = pltpu.make_async_copy(src, dst, in_sem.at[n])
        load.start()
        loads.append(load)

    def device(dy, dx, dc):
        return (lax.rem(y + dy, 4) * 4 + lax.rem(x + dx, 4)) * 2 + lax.rem(core + dc, 2)

    def greet(sem, grp, dev):
        pl.semaphore_signal(sem, 1, device_id={"grp": grp, "dev": dev}, device_id_type=MESH)

    barrier = pltpu.get_barrier_semaphore()
    row = [(0, dx, dc) for dx in (2, 1, 3, 0) for dc in range(2) if dx or dc]
    column = [(dy, 0, 0) for dy in (2, 1, 3)]
    for move in row + column:
        greet(barrier, g, device(*move))

    @pl.when(late == 0)
    def _():
        for step in [8] + [s for n in range(7, 0, -1) for s in (n, GRP - n)]:
            greet(barrier, lax.rem(g + step, GRP), d)

    def for_late(deltas, act):
        for delta in deltas:
            @pl.when((late == 1) & (g + delta >= HALF) & (g + delta < GRP))
            def _(delta=delta):
                act(g + delta)

    for_late((-2, 2, -1, 1), lambda to: greet(barrier, to, d))

    for load in loads:
        load.wait()
    packed = pack(pos_ref[...], frc_ref[...], vol_ref[...], bin_ref[...], elem_ref[...])
    send1[...] = packed.reshape(send1.shape)

    below, above = g - HALF, GRP - 1 - g
    greeted = late * (1 + jnp.minimum(below, 2) + jnp.minimum(above, 2))
    pl.semaphore_wait(barrier, len(row) + len(column) + HALF - 1 + greeted)

    def send_grp(to):
        pltpu.make_async_remote_copy(
            src_ref=send1.at[to],
            dst_ref=recv1.at[g],
            send_sem=send1_sem,
            recv_sem=recv1_sem,
            device_id={"grp": to, "dev": d},
            device_id_type=MESH,
        ).start()

    @pl.when(late == 0)
    def _():
        for step in range(1, HALF):
            send_grp(lax.rem(g + step, HALF))

    @pl.when(late == 1)
    def _():
        for n in range(HALF):
            send_grp(n)
        for n in range(HALF):
            greet(late_sem, n, d)

    for_late((-2, 2), lambda to: greet(near_sem, to, d))
    for_late((-2, 2, -1, 1), send_grp)
    for move in column:
        greet(dev_sem, g, device(*move))
    acc[...] = jnp.zeros_like(acc)
    recv1[g] = send1[g]

    @pl.when(late == 0)
    def _():
        pl.semaphore_wait(late_sem, HALF)
        for n in range(HALF):
            send_grp(HALF + n)

    @pl.when(late == 1)
    def _():
        pl.semaphore_wait(near_sem, jnp.minimum(below // 2, 1) + jnp.minimum(above // 2, 1))

    for_late((-4, 4), lambda to: greet(far_sem, to, d))
    for_late((-4, 4, -3, 3), send_grp)

    @pl.when(late == 1)
    def _():
        pl.semaphore_wait(far_sem, 1)

    for_late((-7, 7, -6, 6, -5, 5), send_grp)

    pl.semaphore_wait(dev_sem, len(column))
    others = recv1.at[pl.ds(0, GRP - 1)]
    pltpu.make_async_copy(others, others, recv1_sem).wait()

    tiles = to_dev_tiles([recv1[v] for v in range(16)])
    send2[...] = jnp.concatenate(tiles, axis=0).reshape(send2.shape)
    slot = core * 16 + d // 2
    for n in range(15, -1, -1):
        dy, dx = CHIPS[n]
        for dc in range(2):
            if n or dc:
                peer = device((4 - dy) % 4, (4 - dx) % 4, dc)
                pltpu.make_async_remote_copy(
                    src_ref=send2.at[peer],
                    dst_ref=recv2.at[slot],
                    send_sem=send2_sem,
                    recv_sem=recv2_sem.at[(1 - core) * (1 + n // 8)],
                    device_id={"grp": g, "dev": peer},
                    device_id_type=MESH,
                ).start()
    recv2[slot] = send2[d]

    def await_chunk(n, count):
        part = recv2.at[pl.ds(0, count)]
        pltpu.make_async_copy(part, part, recv2_sem.at[n]).wait()

    def await_others(n, count, mine):
        @pl.when(mine)
        def _():
            await_chunk(n, count - 1)

        @pl.when(jnp.logical_not(mine))
        def _():
            await_chunk(n, count)

    def near(n):
        dy, dx = CHIPS[n]
        return recv2[lax.rem(y + dy, 4) * 4 + lax.rem(x + dx, 4)]

    def project(pairs):
        tiles = [swap_halves(jnp.concatenate(pair, axis=0)) for pair in pairs]
        return slabs(jnp.concatenate(tiles, axis=1))

    await_others(0, 16, core == 1)
    acc[...] = project([(recv2[16 + n], recv2[17 + n]) for n in range(0, 16, 2)])
    await_others(1, 8, core == 0)
    acc[...] += project([(near(n), near(n + 1)) for n in range(0, 8, 2)])
    await_chunk(2, 8)
    raw = acc[...] + project([(near(n), near(n + 1)) for n in range(8, 16, 2)])
    raw0, raw5 = raw[0:144], raw[720:864]
    out_ref[144:720, :] = raw[144:720]
    sub, lane = iota((8, TILE), 0), iota((8, TILE), 1)
    to_prev, to_next = jnp.zeros((8, TILE), F32), jnp.zeros((8, TILE), F32)
    for b in range(18):
        to_prev = jnp.where(lane == b, roll(raw0[8 * b:8 * b + 8], b, 1), to_prev)
        to_next = jnp.where(lane == b, roll(raw5[8 * b:8 * b + 8], b + 1, 1), to_next)
    rim_out[0] = to_prev
    rim_out[1] = to_next
    me = g * DEV + d
    ends = []
    for way, step in ((0, GRP * DEV - 1), (1, 1)):
        to = lax.rem(me + step, GRP * DEV)
        end = pltpu.make_async_remote_copy(
            src_ref=rim_out.at[way],
            dst_ref=rim_in.at[way],
            send_sem=rim_send_sem.at[way],
            recv_sem=rim_recv_sem.at[way],
            device_id={"grp": to // DEV, "dev": lax.rem(to, DEV)},
            device_id_type=MESH,
        )
        end.start()
        ends.append(end)

    for end in ends:
        end.wait()
    from_next = jnp.where(me == GRP * DEV - 1, 0.0, rim_in[0])
    from_prev = jnp.where(me == 0, 0.0, rim_in[1])
    out5, out0 = [], []
    for b in range(18):
        block0, block5 = raw0[8 * b:8 * b + 8], raw5[8 * b:8 * b + 8]
        after = jnp.where(lane == TILE - 1, roll(from_next, TILE - 1 - b, 1), roll(block0, -1, 1))
        before = jnp.where(lane == 0, roll(from_prev, -b, 1), roll(block5, 1, 1))
        out5.append(block5 + after)
        out0.append(block0 + before)
    out_ref[0:144, :] = jnp.concatenate(out0, axis=0)
    out_ref[720:864, :] = jnp.concatenate(out5, axis=0)

    sent1 = send1.at[pl.ds(0, GRP - 1)]
    pltpu.make_async_copy(sent1, sent1, send1_sem).wait()
    sent2 = send2.at[pl.ds(0, DEV - 1)]
    pltpu.make_async_copy(sent2, sent2, send2_sem).wait()


def interleave(raw_ref, out_ref):
    for k in range(6):
        out_ref[pl.ds(k, 144, stride=6), :] = raw_ref[pl.ds(144 * k, 144), :]


def per_device(positions, forces, volumes, dest_bin, element):
    vmem = pl.BlockSpec(memory_space=pltpu.VMEM)
    dma, regular = pltpu.SemaphoreType.DMA, pltpu.SemaphoreType.REGULAR
    raw = pl.pallas_call(
        kernel,
        out_shape=pltpu.VMEM((864, ELEMS), F32),
        in_specs=[pl.BlockSpec(memory_space=pl.ANY)] * 5,
        out_specs=vmem,
        scratch_shapes=[
            pltpu.VMEM((3, LOCAL), F32),
            pltpu.VMEM((3, LOCAL), F32),
            pltpu.VMEM((1, LOCAL), F32),
            pltpu.VMEM((1, LOCAL), I32),
            pltpu.VMEM((1, LOCAL), I32),
            pltpu.VMEM((GRP, 8, TILE), F32),
            pltpu.VMEM((GRP, 8, TILE), F32),
            pltpu.VMEM((DEV, 4, TILE), F32),
            pltpu.VMEM((DEV, 4, TILE), F32),
            pltpu.VMEM((864, ELEMS), F32),
            pltpu.VMEM((2, 8, TILE), F32),
            pltpu.VMEM((2, 8, TILE), F32),
            dma((5,)), dma, dma, dma, dma((3,)), regular, regular, regular, regular,
            dma((2,)), dma((2,)),
        ],
        compiler_params=pltpu.CompilerParams(collective_id=0, has_side_effects=True),
        name="project",
    )(
        positions,
        forces,
        volumes.reshape(1, LOCAL),
        dest_bin.reshape(1, LOCAL),
        element.reshape(1, LOCAL),
    )
    out = pl.pallas_call(
        interleave,
        out_shape=jax.ShapeDtypeStruct((864, ELEMS), F32),
        in_specs=[vmem],
        out_specs=vmem,
        name="interleave",
    )(pltpu.with_memory_space_constraint(raw, pltpu.VMEM))
    return out.reshape(4, 216, ELEMS)


def solution(mesh):
    in_specs = (
        P(None, ("grp", "dev")),
        P(None, ("grp", "dev")),
        P(("grp", "dev")),
        P(("grp", "dev"), None),
        P(("grp", "dev")),
    )
    out_specs = P(None, None, ("grp", "dev"))
    return jax.shard_map(
        per_device, mesh=mesh, in_specs=in_specs, out_specs=out_specs, check_vma=False
    )
```

```python
import functools

import jax
import jax.numpy as jnp
from jax import lax
from jax.experimental import pallas as pl
from jax.experimental.pallas import tpu as pltpu
from jax.sharding import PartitionSpec as P

MESH = pl.DeviceIdType.MESH
F32, BF16, I32 = jnp.float32, jnp.bfloat16, jnp.int32

GRP, DEV, SLOTS, LOCAL, ELEMS = 16, 32, 4, 1024, 128
TILE = 128
HALF = 8

gll_points = (
    -1.0,
    -0.765055323929465,
    -0.285231516480645,
    0.285231516480645,
    0.765055323929465,
    1.0,
)


def iota(shape, axis):
    return lax.broadcasted_iota(I32, shape, axis)


def roll(x, shift, axis):
    shift = shift % x.shape[axis]
    return x if shift == 0 else pltpu.roll(x, shift, axis)


def dot_nt(a, b):
    return lax.dot_general(a, b, (((1,), (1,)), ((), ())), preferred_element_type=F32)


def rank_in_bin(target):
    blocks = LOCAL // TILE
    row = target.astype(F32)
    parts = [row[:, b * TILE:(b + 1) * TILE] for b in range(blocks)]
    columns = [jnp.transpose(jnp.broadcast_to(part, (TILE, TILE))) for part in parts]
    earlier = iota((TILE, TILE), 0) < iota((TILE, TILE), 1)
    ranks = []
    for p in range(blocks):
        own = (columns[p] == parts[p]) & earlier
        total = jnp.where(own, 1.0, 0.0)
        for q in range(p):
            total = total + jnp.where(columns[q] == parts[p], 1.0, 0.0)
        ranks.append(jnp.sum(total, axis=0, keepdims=True))
    return jnp.concatenate(ranks, axis=1).astype(I32)


def pieces(x):
    high = x.astype(BF16).astype(F32)
    rest = x - high
    mid = rest.astype(BF16).astype(F32)
    return high, mid, rest - mid


def pack(positions, forces, volumes, target, element):
    dev = target % DEV
    code = (dev % 2) * 64 + (dev // 2) * SLOTS + rank_in_bin(target)
    row_of = iota((TILE, LOCAL), 0)
    mine = (row_of // 8) == target // DEV
    sub = iota((8, LOCAL), 0)
    parts = [positions[n:n + 1] for n in range(3)] + [element.astype(F32)]
    parts += [forces[n:n + 1] for n in range(3)] + [volumes]
    feats = parts[7]
    for n in range(7):
        feats = jnp.where(sub == n, parts[n], feats)
    left = jnp.concatenate(
        [
            jnp.where(mine, jnp.concatenate([piece] * 16, axis=0), 0.0).astype(BF16)
            for piece in pieces(feats)
        ],
        axis=0,
    )
    right = jnp.where(row_of == code, 1.0, 0.0).astype(BF16)
    prod = dot_nt(left, right)
    return prod[0:128] + prod[128:256] + prod[256:384]


def swap_halves(x):
    sub, lane = iota((8, TILE), 0), iota((8, TILE), 1)
    return jnp.where((sub // 4) == (lane // 64), x, roll(roll(x, 4, 0), 64, 1))


def to_dev_tiles(tiles):
    lane = iota((8, TILE), 1)
    for bit in range(4):
        step = 4 << bit
        low = (lane // step) % 2 == 0
        new = list(tiles)
        for v in range(16):
            if not (v >> bit) & 1:
                a, b = tiles[v], tiles[v | (1 << bit)]
                new[v] = jnp.where(low, a, roll(b, step, 1))
                new[v | (1 << bit)] = jnp.where(low, roll(a, -step, 1), b)
        tiles = new
    return [swap_halves(x) for x in tiles]


def by_row(sub, labels, parts):
    out = parts[labels[0]]
    for s in range(1, 8):
        if labels[s] != labels[s - 1]:
            out = jnp.where(sub >= s, parts[labels[s]], out)
    return out


def weigh(x):
    width = x.shape[1]
    shape = (8, width)
    sub = iota(shape, 0)
    nodes = jnp.full(shape, gll_points[5], F32)
    for n in range(5):
        nodes = jnp.where(sub == n, gll_points[n], nodes)
    w_r, w_s, w_t = [jnp.exp(-((nodes - x[d:d + 1]) ** 2) / 0.5) for d in range(3)]
    r_rows = [jnp.broadcast_to(w_r[i:i + 1], shape) for i in range(6)]
    s_cycle = (
        jnp.where(sub < 6, w_s, roll(w_s, 6, 0)),
        jnp.where(sub < 4, roll(w_s, 6, 0), roll(w_s, 4, 0)),
        jnp.where(sub < 2, roll(w_s, 4, 0), roll(w_s, 2, 0)),
    )
    faces = [
        by_row(sub, [((8 * b + s) % 36) // 6 for s in range(8)], r_rows) * s_cycle[b % 3]
        for b in range(9)
    ]
    values = [jnp.broadcast_to(x[d:d + 1], shape) for d in (7, 4, 5, 6)]
    scaled = [
        by_row(sub, [(8 * b + s) // 36 for s in range(8)], values) * faces[b % 9]
        for b in range(18)
    ]
    return scaled, w_t


def slabs(x):
    scaled, w_t = weigh(x)
    onehot = jnp.where(iota((ELEMS, x.shape[1]), 0) == x[3:4].astype(I32), 1.0, 0.0).astype(BF16)
    rows = []
    for k in range(6):
        weight = jnp.broadcast_to(w_t[k:k + 1], scaled[0].shape)
        rows += [part * weight for part in scaled]
    return dot_nt(jnp.concatenate(rows, axis=0).astype(BF16), onehot)


def face_sums(tiles):
    x = jnp.concatenate(tiles, axis=1)
    scaled, w_t = weigh(x)
    first, last = x[3:4] == 0.0, x[3:4] == ELEMS - 1.0
    weight = jnp.where(first, w_t[0:1], jnp.where(last, w_t[5:6], 0.0))
    weight = jnp.broadcast_to(weight, scaled[0].shape)
    rows = [part * weight for part in scaled]
    fill = [jnp.zeros_like(weight)] * 7
    rank, lane = iota((TILE, TILE), 0), iota((TILE, TILE), 1)
    owner = ((lane // 4) % 16) * 2 + lane // 64
    side = rank % 2
    match = owner == (rank // 4 + 1 + 30 * side) % DEV
    firsts, lasts = jnp.where(first, 1.0, 0.0), jnp.where(last, 1.0, 0.0)
    chosen = jnp.concatenate(
        [
            jnp.where(
                match & (side == 0),
                firsts[:, t:t + TILE],
                jnp.where(match & (side == 1), lasts[:, t:t + TILE], 0.0),
            )
            for t in range(0, x.shape[1], TILE)
        ],
        axis=1,
    ).astype(BF16)
    halves = [
        dot_nt(chosen, jnp.concatenate(rows[h:h + 9] + fill, axis=0).astype(BF16)) for h in (0, 9)
    ]
    return jnp.where(rank % 4 < 2, halves[0], halves[1])


CHIPS = sorted(
    [(dy, dx) for dy in range(4) for dx in range(4)],
    key=lambda m: min(m[0], 4 - m[0]) + min(m[1], 4 - m[1]),
)


def kernel(
    pos_hbm, frc_hbm, vol_hbm, bin_hbm, elem_hbm, out_ref,
    pos_ref, frc_ref, vol_ref, bin_ref, elem_ref,
    send1, recv1, send2, recv2, acc, send3, recv3, recv3x, rim,
    in_sem, send1_sem, recv1_sem, send2_sem, recv2_sem, late_sem, near_sem, far_sem, dev_sem,
    slab_sem, send3_sem, recv3_sem, send3x_sem, recv3x_sem,
):
    g, d = lax.axis_index("grp"), lax.axis_index("dev")
    y, x, core = d // 8, (d // 2) % 4, d % 2
    late = g // HALF

    loads = []
    for n, (src, dst) in enumerate((
        (bin_hbm, bin_ref), (pos_hbm, pos_ref), (frc_hbm, frc_ref),
        (vol_hbm, vol_ref), (elem_hbm, elem_ref),
    )):
        load = pltpu.make_async_copy(src, dst, in_sem.at[n])
        load.start()
        loads.append(load)

    def device(dy, dx, dc):
        return (lax.rem(y + dy, 4) * 4 + lax.rem(x + dx, 4)) * 2 + lax.rem(core + dc, 2)

    def greet(sem, grp, dev):
        pl.semaphore_signal(sem, 1, device_id={"grp": grp, "dev": dev}, device_id_type=MESH)

    barrier = pltpu.get_barrier_semaphore()
    row = [(0, dx, dc) for dx in (2, 1, 3, 0) for dc in range(2) if dx or dc]
    column = [(dy, 0, 0) for dy in (2, 1, 3)]
    for move in row + column:
        greet(barrier, g, device(*move))

    @pl.when(late == 0)
    def _():
        for step in [8] + [s for n in range(7, 0, -1) for s in (n, GRP - n)]:
            greet(barrier, lax.rem(g + step, GRP), d)

    def for_late(deltas, act):
        for delta in deltas:
            @pl.when((late == 1) & (g + delta >= HALF) & (g + delta < GRP))
            def _(delta=delta):
                act(g + delta)

    for_late((-2, 2, -1, 1), lambda to: greet(barrier, to, d))

    for load in loads:
        load.wait()
    packed = pack(pos_ref[...], frc_ref[...], vol_ref[...], bin_ref[...], elem_ref[...])
    send1[...] = packed.reshape(send1.shape)

    below, above = g - HALF, GRP - 1 - g
    greeted = late * (1 + jnp.minimum(below, 2) + jnp.minimum(above, 2))
    pl.semaphore_wait(barrier, len(row) + len(column) + HALF - 1 + greeted)

    def send_grp(to):
        pltpu.make_async_remote_copy(
            src_ref=send1.at[to],
            dst_ref=recv1.at[g],
            send_sem=send1_sem,
            recv_sem=recv1_sem,
            device_id={"grp": to, "dev": d},
            device_id_type=MESH,
        ).start()

    @pl.when(late == 0)
    def _():
        for step in range(1, HALF):
            send_grp(lax.rem(g + step, HALF))

    @pl.when(late == 1)
    def _():
        for n in range(HALF):
            send_grp(n)
        for n in range(HALF):
            greet(late_sem, n, d)

    for_late((-2, 2), lambda to: greet(near_sem, to, d))
    for_late((-2, 2, -1, 1), send_grp)
    for move in column:
        greet(dev_sem, g, device(*move))
    recv1[g] = send1[g]

    @pl.when(late == 0)
    def _():
        pl.semaphore_wait(late_sem, HALF)
        for n in range(HALF):
            send_grp(HALF + n)

    @pl.when(late == 1)
    def _():
        pl.semaphore_wait(near_sem, jnp.minimum(below // 2, 1) + jnp.minimum(above // 2, 1))

    for_late((-4, 4), lambda to: greet(far_sem, to, d))
    for_late((-4, 4, -3, 3), send_grp)

    @pl.when(late == 1)
    def _():
        pl.semaphore_wait(far_sem, 1)

    for_late((-7, 7, -6, 6, -5, 5), send_grp)

    pl.semaphore_wait(dev_sem, len(column))

    @pl.when(g > 0)
    def _():
        greet(slab_sem, g - 1, d)

    @pl.when(g < GRP - 1)
    def _():
        greet(slab_sem, g + 1, d)

    others = recv1.at[pl.ds(0, GRP - 1)]
    pltpu.make_async_copy(others, others, recv1_sem).wait()

    arrived = [recv1[v] for v in range(16)]
    tiles = to_dev_tiles(arrived)
    send2[...] = jnp.concatenate(tiles, axis=0).reshape(send2.shape)
    slot = core * 16 + d // 2
    others = [
        (n, device((4 - CHIPS[n][0]) % 4, (4 - CHIPS[n][1]) % 4, dc))
        for n in range(15, -1, -1) for dc in range(2) if n or dc
    ]
    for n, peer in others:
        pltpu.make_async_remote_copy(
            src_ref=send2.at[peer],
            dst_ref=recv2.at[slot],
            send_sem=send2_sem,
            recv_sem=recv2_sem.at[(1 - core) * (1 + n // 8)],
            device_id={"grp": g, "dev": peer},
            device_id_type=MESH,
        ).start()
    recv2[slot] = send2[d]

    send3[...] = face_sums(arrived).reshape(send3.shape)
    for _, peer in others:
        pltpu.make_async_remote_copy(
            src_ref=send3.at[peer],
            dst_ref=recv3.at[d],
            send_sem=send3_sem,
            recv_sem=recv3_sem,
            device_id={"grp": g, "dev": peer},
            device_id_type=MESH,
        ).start()
    recv3[d] = send3[d]
    pl.semaphore_wait(slab_sem, jnp.minimum(g, 1) + jnp.minimum(GRP - 1 - g, 1))

    def to_slab(n, grp, dev):
        return pltpu.make_async_remote_copy(
            src_ref=send3.at[dev],
            dst_ref=recv3x.at[d],
            send_sem=send3x_sem.at[n],
            recv_sem=recv3x_sem,
            device_id={"grp": grp, "dev": dev},
            device_id_type=MESH,
        )

    @pl.when(g > 0)
    def _():
        to_slab(0, g - 1, DEV - 1).start()

    @pl.when(g < GRP - 1)
    def _():
        to_slab(1, g + 1, 0).start()

    def await_chunk(n, count):
        part = recv2.at[pl.ds(0, count)]
        pltpu.make_async_copy(part, part, recv2_sem.at[n]).wait()

    def await_others(n, count, mine):
        @pl.when(mine)
        def _():
            await_chunk(n, count - 1)

        @pl.when(jnp.logical_not(mine))
        def _():
            await_chunk(n, count)

    def near(n):
        dy, dx = CHIPS[n]
        return recv2[lax.rem(y + dy, 4) * 4 + lax.rem(x + dx, 4)]

    def project(pairs):
        tiles = [swap_halves(jnp.concatenate(pair, axis=0)) for pair in pairs]
        return slabs(jnp.concatenate(tiles, axis=1))

    await_others(0, 16, core == 1)
    acc[...] = project([(recv2[16 + n], recv2[17 + n]) for n in range(0, 16, 2)])
    await_others(1, 8, core == 0)
    acc[...] += project([(near(n), near(n + 1)) for n in range(0, 8, 2)])
    await_chunk(2, 8)
    raw = acc[...] + project([(near(n), near(n + 1)) for n in range(8, 16, 2)])
    raw0, raw5 = raw[0:144], raw[720:864]
    out_ref[144:720, :] = raw[144:720]

    rest = recv3.at[pl.ds(0, DEV - 1)]
    pltpu.make_async_copy(rest, rest, recv3_sem).wait()
    side = iota((4, TILE), 0) % 2
    keep = jnp.where(side == 0, jnp.minimum(DEV - 1 - d, 1), jnp.minimum(d, 1)).astype(F32)
    rim[...] = jnp.zeros_like(rim)
    rim[0:4, :] = keep * jnp.sum(recv3[...], axis=0)

    def add_slab(of):
        pltpu.make_async_copy(recv3x, recv3x, recv3x_sem).wait()
        rim[0:4, :] += jnp.where(side == of, jnp.sum(recv3x[...], axis=0), 0.0)

    @pl.when((d == DEV - 1) & (g < GRP - 1))
    def _():
        add_slab(0)

    @pl.when((d == 0) & (g > 0))
    def _():
        add_slab(1)

    columns = jnp.transpose(jnp.concatenate([rim[...], jnp.zeros((TILE - 8, TILE), F32)], axis=0))
    lane = iota((8, TILE), 1)
    out5, out0 = [], []
    for b in range(18):
        block0, block5 = raw0[8 * b:8 * b + 8], raw5[8 * b:8 * b + 8]
        faces, half = columns[8 * (b % 9):8 * (b % 9) + 8], 2 * (b // 9)
        after = jnp.where(lane == TILE - 1, roll(faces, TILE - 1 - half, 1), roll(block0, -1, 1))
        before = jnp.where(lane == 0, roll(faces, -1 - half, 1), roll(block5, 1, 1))
        out5.append(block5 + after)
        out0.append(block0 + before)
    out_ref[0:144, :] = jnp.concatenate(out0, axis=0)
    out_ref[720:864, :] = jnp.concatenate(out5, axis=0)

    sent1 = send1.at[pl.ds(0, GRP - 1)]
    pltpu.make_async_copy(sent1, sent1, send1_sem).wait()
    sent2 = send2.at[pl.ds(0, DEV - 1)]
    pltpu.make_async_copy(sent2, sent2, send2_sem).wait()
    sent3 = send3.at[pl.ds(0, DEV - 1)]
    pltpu.make_async_copy(sent3, sent3, send3_sem).wait()

    @pl.when(g > 0)
    def _():
        to_slab(0, g - 1, DEV - 1).wait_send()

    @pl.when(g < GRP - 1)
    def _():
        to_slab(1, g + 1, 0).wait_send()


def interleave(raw_ref, out_ref):
    for k in range(6):
        out_ref[pl.ds(k, 144, stride=6), :] = raw_ref[pl.ds(144 * k, 144), :]


def per_device(positions, forces, volumes, dest_bin, element):
    vmem = pl.BlockSpec(memory_space=pltpu.VMEM)
    dma, regular = pltpu.SemaphoreType.DMA, pltpu.SemaphoreType.REGULAR
    raw = pl.pallas_call(
        kernel,
        out_shape=pltpu.VMEM((864, ELEMS), F32),
        in_specs=[pl.BlockSpec(memory_space=pl.ANY)] * 5,
        out_specs=vmem,
        scratch_shapes=[
            pltpu.VMEM((3, LOCAL), F32),
            pltpu.VMEM((3, LOCAL), F32),
            pltpu.VMEM((1, LOCAL), F32),
            pltpu.VMEM((1, LOCAL), I32),
            pltpu.VMEM((1, LOCAL), I32),
            pltpu.VMEM((GRP, 8, TILE), F32),
            pltpu.VMEM((GRP, 8, TILE), F32),
            pltpu.VMEM((DEV, 4, TILE), F32),
            pltpu.VMEM((DEV, 4, TILE), F32),
            pltpu.VMEM((864, ELEMS), F32),
            pltpu.VMEM((DEV, 4, TILE), F32),
            pltpu.VMEM((DEV, 4, TILE), F32),
            pltpu.VMEM((DEV, 4, TILE), F32),
            pltpu.VMEM((8, TILE), F32),
            dma((5,)), dma, dma, dma, dma((3,)), regular, regular, regular, regular,
            regular, dma, dma, dma((2,)), dma,
        ],
        compiler_params=pltpu.CompilerParams(collective_id=0, has_side_effects=True),
        name="project",
    )(
        positions,
        forces,
        volumes.reshape(1, LOCAL),
        dest_bin.reshape(1, LOCAL),
        element.reshape(1, LOCAL),
    )
    out = pl.pallas_call(
        interleave,
        out_shape=jax.ShapeDtypeStruct((864, ELEMS), F32),
        in_specs=[vmem],
        out_specs=vmem,
        name="interleave",
    )(pltpu.with_memory_space_constraint(raw, pltpu.VMEM))
    return out.reshape(4, 216, ELEMS)


def solution(mesh):
    in_specs = (
        P(None, ("grp", "dev")),
        P(None, ("grp", "dev")),
        P(("grp", "dev")),
        P(("grp", "dev"), None),
        P(("grp", "dev")),
    )
    out_specs = P(None, None, ("grp", "dev"))
    return jax.shard_map(
        per_device, mesh=mesh, in_specs=in_specs, out_specs=out_specs, check_vma=False
    )
```

```python
import functools

import jax
import jax.numpy as jnp
from jax import lax
from jax.experimental import pallas as pl
from jax.experimental.pallas import tpu as pltpu
from jax.sharding import PartitionSpec as P

MESH = pl.DeviceIdType.MESH
F32, BF16, I32 = jnp.float32, jnp.bfloat16, jnp.int32

GRP, DEV, SLOTS, LOCAL, ELEMS = 16, 32, 4, 1024, 128
TILE = 128
EARLY, LATE = 6, 10
BOUNDS = (10,)

gll_points = (
    -1.0,
    -0.765055323929465,
    -0.285231516480645,
    0.285231516480645,
    0.765055323929465,
    1.0,
)


def iota(shape, axis):
    return lax.broadcasted_iota(I32, shape, axis)


def roll(x, shift, axis):
    shift = shift % x.shape[axis]
    return x if shift == 0 else pltpu.roll(x, shift, axis)


def dot_nt(a, b):
    return lax.dot_general(a, b, (((1,), (1,)), ((), ())), preferred_element_type=F32)


def rank_in_bin(target):
    blocks = LOCAL // TILE
    row = target.astype(F32)
    parts = [row[:, b * TILE:(b + 1) * TILE] for b in range(blocks)]
    columns = [jnp.transpose(jnp.broadcast_to(part, (TILE, TILE))) for part in parts]
    earlier = iota((TILE, TILE), 0) < iota((TILE, TILE), 1)
    ranks = []
    for p in range(blocks):
        own = (columns[p] == parts[p]) & earlier
        total = jnp.where(own, 1.0, 0.0)
        for q in range(p):
            total = total + jnp.where(columns[q] == parts[p], 1.0, 0.0)
        ranks.append(jnp.sum(total, axis=0, keepdims=True))
    return jnp.concatenate(ranks, axis=1).astype(I32)


def pieces(x):
    high = x.astype(BF16).astype(F32)
    rest = x - high
    mid = rest.astype(BF16).astype(F32)
    return high, mid, rest - mid


def pack(positions, forces, volumes, target, element):
    dev = target % DEV
    code = (dev % 2) * 64 + (dev // 2) * SLOTS + rank_in_bin(target)
    row_of = iota((TILE, LOCAL), 0)
    mine = (row_of // 8) == target // DEV
    sub = iota((8, LOCAL), 0)
    parts = [positions[n:n + 1] for n in range(3)] + [element.astype(F32)]
    parts += [forces[n:n + 1] for n in range(3)] + [volumes]
    feats = parts[7]
    for n in range(7):
        feats = jnp.where(sub == n, parts[n], feats)
    left = jnp.concatenate(
        [
            jnp.where(mine, jnp.concatenate([piece] * 16, axis=0), 0.0).astype(BF16)
            for piece in pieces(feats)
        ],
        axis=0,
    )
    right = jnp.where(row_of == code, 1.0, 0.0).astype(BF16)
    prod = dot_nt(left, right)
    return prod[0:128] + prod[128:256] + prod[256:384]


def swap_halves(x):
    sub, lane = iota((8, TILE), 0), iota((8, TILE), 1)
    return jnp.where((sub // 4) == (lane // 64), x, roll(roll(x, 4, 0), 64, 1))


def to_dev_tiles(tiles):
    lane = iota((8, TILE), 1)
    for bit in range(4):
        step = 4 << bit
        low = (lane // step) % 2 == 0
        new = list(tiles)
        for v in range(16):
            if not (v >> bit) & 1:
                a, b = tiles[v], tiles[v | (1 << bit)]
                new[v] = jnp.where(low, a, roll(b, step, 1))
                new[v | (1 << bit)] = jnp.where(low, roll(a, -step, 1), b)
        tiles = new
    return [swap_halves(x) for x in tiles]


def by_row(sub, labels, parts):
    out = parts[labels[0]]
    for s in range(1, 8):
        if labels[s] != labels[s - 1]:
            out = jnp.where(sub >= s, parts[labels[s]], out)
    return out


def weigh(x):
    width = x.shape[1]
    shape = (8, width)
    sub = iota(shape, 0)
    nodes = jnp.full(shape, gll_points[5], F32)
    for n in range(5):
        nodes = jnp.where(sub == n, gll_points[n], nodes)
    w_r, w_s, w_t = [jnp.exp(-((nodes - x[d:d + 1]) ** 2) / 0.5) for d in range(3)]
    r_rows = [jnp.broadcast_to(w_r[i:i + 1], shape) for i in range(6)]
    s_cycle = (
        jnp.where(sub < 6, w_s, roll(w_s, 6, 0)),
        jnp.where(sub < 4, roll(w_s, 6, 0), roll(w_s, 4, 0)),
        jnp.where(sub < 2, roll(w_s, 4, 0), roll(w_s, 2, 0)),
    )
    faces = [
        by_row(sub, [((8 * b + s) % 36) // 6 for s in range(8)], r_rows) * s_cycle[b % 3]
        for b in range(9)
    ]
    values = [jnp.broadcast_to(x[d:d + 1], shape) for d in (7, 4, 5, 6)]
    scaled = [
        by_row(sub, [(8 * b + s) // 36 for s in range(8)], values) * faces[b % 9]
        for b in range(18)
    ]
    return scaled, w_t


def slabs(x):
    scaled, w_t = weigh(x)
    onehot = jnp.where(iota((ELEMS, x.shape[1]), 0) == x[3:4].astype(I32), 1.0, 0.0).astype(BF16)
    rows = []
    for k in range(6):
        weight = jnp.broadcast_to(w_t[k:k + 1], scaled[0].shape)
        rows += [part * weight for part in scaled]
    return dot_nt(jnp.concatenate(rows, axis=0).astype(BF16), onehot)


def face_sums(tiles):
    x = jnp.concatenate(tiles, axis=1)
    scaled, w_t = weigh(x)
    first, last = x[3:4] == 0.0, x[3:4] == ELEMS - 1.0
    weight = jnp.where(first, w_t[0:1], jnp.where(last, w_t[5:6], 0.0))
    weight = jnp.broadcast_to(weight, scaled[0].shape)
    rows = [part * weight for part in scaled]
    fill = [jnp.zeros_like(weight)] * 7
    rank, lane = iota((TILE, TILE), 0), iota((TILE, TILE), 1)
    owner = ((lane // 4) % 16) * 2 + lane // 64
    side = rank % 2
    match = owner == (rank // 4 + 1 + 30 * side) % DEV
    firsts, lasts = jnp.where(first, 1.0, 0.0), jnp.where(last, 1.0, 0.0)
    chosen = jnp.concatenate(
        [
            jnp.where(
                match & (side == 0),
                firsts[:, t:t + TILE],
                jnp.where(match & (side == 1), lasts[:, t:t + TILE], 0.0),
            )
            for t in range(0, x.shape[1], TILE)
        ],
        axis=1,
    ).astype(BF16)
    halves = [
        dot_nt(chosen, jnp.concatenate(rows[h:h + 9] + fill, axis=0).astype(BF16)) for h in (0, 9)
    ]
    return jnp.where(rank % 4 < 2, halves[0], halves[1])


CHIPS = sorted(
    [(dy, dx) for dy in range(4) for dx in range(4)],
    key=lambda m: min(m[0], 4 - m[0]) + min(m[1], 4 - m[1]),
)


def kernel(
    pos_hbm, frc_hbm, vol_hbm, bin_hbm, elem_hbm, out_ref,
    pos_ref, frc_ref, vol_ref, bin_ref, elem_ref,
    send1, recv1, send2, recv2, acc, send3, recv3, recv3x, rim,
    in_sem, send1_sem, recv1_sem, send2_sem, recv2_sem, late_sem, near_sem,
    slab_sem, chain_sem, send3_sem, recv3_sem, send3x_sem, recv3x_sem,
):
    g, d = lax.axis_index("grp"), lax.axis_index("dev")
    y, x, core = d // 8, (d // 2) % 4, d % 2
    late = (g + LATE) // GRP

    loads = []
    for n, (src, dst) in enumerate((
        (bin_hbm, bin_ref), (pos_hbm, pos_ref), (frc_hbm, frc_ref),
        (vol_hbm, vol_ref), (elem_hbm, elem_ref),
    )):
        load = pltpu.make_async_copy(src, dst, in_sem.at[n])
        load.start()
        loads.append(load)

    def device(dy, dx, dc):
        return (lax.rem(y + dy, 4) * 4 + lax.rem(x + dx, 4)) * 2 + lax.rem(core + dc, 2)

    def greet(sem, grp, dev):
        pl.semaphore_signal(sem, 1, device_id={"grp": grp, "dev": dev}, device_id_type=MESH)

    other = d + 1 - 2 * core
    below, above = g - EARLY, GRP - 1 - g
    row = [(0, dx, dc) for dx in (2, 1, 3, 0) for dc in range(2) if dx or dc]
    column = [(2, 0, 0), (1, 0, 0), (3, 0, 0)]

    def only(condition, act):
        @pl.when(condition)
        def _():
            act()

    def greet_moves(sem, moves):
        for move in moves:
            greet(sem, g, device(*move))

    def for_late(deltas, act):
        for delta in deltas:
            inside = (late == 1) & (g + delta >= EARLY) & (g + delta < GRP)
            only(inside, functools.partial(act, g + delta))

    def greet_both(to):
        greet(barrier, to, d)
        greet(barrier, to, other)

    def in_range(delta):
        return jnp.minimum(below // delta, 1) + jnp.minimum(above // delta, 1)

    barrier = pltpu.get_barrier_semaphore()

    def greet_grp():
        for n in range(EARLY):
            only(g != n, functools.partial(greet, barrier, n, other))
        for n in range(LATE):
            greet(barrier, EARLY + n, other)

    greet_moves(barrier, row + column)
    for_late((-2, 2, -1, 1), greet_both)
    only(late == 0, greet_grp)

    for load in loads:
        load.wait()
    packed = pack(pos_ref[...], frc_ref[...], vol_ref[...], bin_ref[...], elem_ref[...])
    send1[...] = packed.reshape(send1.shape)

    greeted = EARLY - 1 + late * (1 + 2 * in_range(1) + 2 * in_range(2))
    pl.semaphore_wait(barrier, len(row) + len(column) + greeted)

    def send_grp(to):
        pltpu.make_async_remote_copy(
            src_ref=send1.at[to],
            dst_ref=recv1.at[g],
            send_sem=send1_sem,
            recv_sem=recv1_sem.at[late],
            device_id={"grp": to, "dev": other},
            device_id_type=MESH,
        ).start()

    def early_sends():
        for n in range(EARLY):
            only(g != n, functools.partial(send_grp, n))
        send_grp(g)
        greet_moves(slab_sem, column)
        pl.semaphore_wait(late_sem, LATE)
        for n in range(LATE):
            send_grp(EARLY + n)

    def late_sends():
        for n in range(EARLY):
            send_grp(n)
        for n in range(EARLY):
            greet(late_sem, n, other)
        for_late((-2, 2), lambda to: greet(near_sem.at[0], to, d))
        greet_moves(slab_sem, column)
        for_late((-2, 2, -1, 1), send_grp)
        send_grp(g)
        pl.semaphore_wait(near_sem.at[0], in_range(2))
        for_late((-4, 4), lambda to: greet(near_sem.at[1], to, d))
        for_late((-4, 4, -3, 3), send_grp)
        pl.semaphore_wait(near_sem.at[1], in_range(4))
        only(g == EARLY + 1, lambda: greet(near_sem.at[2], EARLY, d))
        only(g == GRP - 2, lambda: greet(near_sem.at[2], GRP - 1, d))
        for_late((-8, 8, -7, 7, -6, 6, -5, 5), send_grp)
        only((g == EARLY) | (g == GRP - 1), lambda: pl.semaphore_wait(near_sem.at[2], 1))
        for_late((-9, 9), send_grp)

    only(late == 0, early_sends)
    only(late == 1, late_sends)
    pl.semaphore_wait(slab_sem, len(column))

    only(g > 0, lambda: greet(chain_sem, g - 1, other))
    only(g < GRP - 1, lambda: greet(chain_sem, g + 1, other))

    def await_grp(n, count):
        part = recv1.at[pl.ds(0, count)]
        pltpu.make_async_copy(part, part, recv1_sem.at[n]).wait()

    await_grp(0, EARLY)
    acc[0:TILE, :] = face_sums([recv1[v] for v in range(EARLY)])
    await_grp(1, LATE)
    tiles = to_dev_tiles([recv1[v] for v in range(GRP)])
    send2[...] = jnp.concatenate(tiles, axis=0).reshape(send2.shape)
    others = [
        (n, device((4 - CHIPS[n][0]) % 4, (4 - CHIPS[n][1]) % 4, dc))
        for n in range(15, -1, -1) for dc in range(2) if n or dc
    ]
    for n, peer in others:
        pltpu.make_async_remote_copy(
            src_ref=send2.at[peer],
            dst_ref=recv2.at[d],
            send_sem=send2_sem,
            recv_sem=recv2_sem.at[sum(n >= b for b in BOUNDS)],
            device_id={"grp": g, "dev": peer},
            device_id_type=MESH,
        ).start()
    recv2[d] = send2[d]

    sums = acc[0:TILE, :] + face_sums([recv1[v] for v in range(EARLY, GRP)])
    send3[...] = sums.reshape(send3.shape)
    for _, peer in others:
        pltpu.make_async_remote_copy(
            src_ref=send3.at[peer],
            dst_ref=recv3.at[d],
            send_sem=send3_sem,
            recv_sem=recv3_sem,
            device_id={"grp": g, "dev": peer},
            device_id_type=MESH,
        ).start()
    recv3[d] = send3[d]
    pl.semaphore_wait(chain_sem, jnp.minimum(g, 1) + jnp.minimum(GRP - 1 - g, 1))

    def to_slab(n, grp, dev):
        return pltpu.make_async_remote_copy(
            src_ref=send3.at[dev],
            dst_ref=recv3x.at[d],
            send_sem=send3x_sem.at[n],
            recv_sem=recv3x_sem,
            device_id={"grp": grp, "dev": dev},
            device_id_type=MESH,
        )

    @pl.when(g > 0)
    def _():
        to_slab(0, g - 1, DEV - 1).start()

    @pl.when(g < GRP - 1)
    def _():
        to_slab(1, g + 1, 0).start()

    def await_chunk(n, count):
        part = recv2.at[pl.ds(0, count)]
        pltpu.make_async_copy(part, part, recv2_sem.at[n]).wait()

    def tile(n):
        dy, dx = CHIPS[n]
        first = (lax.rem(y + dy, 4) * 4 + lax.rem(x + dx, 4)) * 2
        return swap_halves(recv2[pl.ds(first, 2)].reshape(8, TILE))

    def project(chips):
        return slabs(jnp.concatenate([tile(n) for n in chips], axis=1))

    raw = None
    for part, (low, high) in enumerate(zip((0,) + BOUNDS, BOUNDS + (16,))):
        await_chunk(part, 2 * (high - low) - (part == 0))
        if raw is not None:
            acc[...] = raw
        raw = project(range(low, high)) + (0.0 if raw is None else acc[...])
    raw0, raw5 = raw[0:144], raw[720:864]
    out_ref[144:720, :] = raw[144:720]

    rest = recv3.at[pl.ds(0, DEV - 1)]
    pltpu.make_async_copy(rest, rest, recv3_sem).wait()
    side = iota((4, TILE), 0) % 2
    keep = jnp.where(side == 0, jnp.minimum(DEV - 1 - d, 1), jnp.minimum(d, 1)).astype(F32)
    rim[...] = jnp.zeros_like(rim)
    rim[0:4, :] = keep * jnp.sum(recv3[...], axis=0)

    def add_slab(of):
        pltpu.make_async_copy(recv3x, recv3x, recv3x_sem).wait()
        rim[0:4, :] += jnp.where(side == of, jnp.sum(recv3x[...], axis=0), 0.0)

    @pl.when((d == DEV - 1) & (g < GRP - 1))
    def _():
        add_slab(0)

    @pl.when((d == 0) & (g > 0))
    def _():
        add_slab(1)

    columns = jnp.transpose(jnp.concatenate([rim[...], jnp.zeros((TILE - 8, TILE), F32)], axis=0))
    lane = iota((8, TILE), 1)
    out5, out0 = [], []
    for b in range(18):
        block0, block5 = raw0[8 * b:8 * b + 8], raw5[8 * b:8 * b + 8]
        faces, half = columns[8 * (b % 9):8 * (b % 9) + 8], 2 * (b // 9)
        after = jnp.where(lane == TILE - 1, roll(faces, TILE - 1 - half, 1), roll(block0, -1, 1))
        before = jnp.where(lane == 0, roll(faces, -1 - half, 1), roll(block5, 1, 1))
        out5.append(block5 + after)
        out0.append(block0 + before)
    out_ref[0:144, :] = jnp.concatenate(out0, axis=0)
    out_ref[720:864, :] = jnp.concatenate(out5, axis=0)

    pltpu.make_async_copy(send1, send1, send1_sem).wait()
    sent2 = send2.at[pl.ds(0, DEV - 1)]
    pltpu.make_async_copy(sent2, sent2, send2_sem).wait()
    sent3 = send3.at[pl.ds(0, DEV - 1)]
    pltpu.make_async_copy(sent3, sent3, send3_sem).wait()

    @pl.when(g > 0)
    def _():
        to_slab(0, g - 1, DEV - 1).wait_send()

    @pl.when(g < GRP - 1)
    def _():
        to_slab(1, g + 1, 0).wait_send()


def interleave(raw_ref, out_ref):
    for k in range(6):
        out_ref[pl.ds(k, 144, stride=6), :] = raw_ref[pl.ds(144 * k, 144), :]


def per_device(positions, forces, volumes, dest_bin, element):
    vmem = pl.BlockSpec(memory_space=pltpu.VMEM)
    dma, regular = pltpu.SemaphoreType.DMA, pltpu.SemaphoreType.REGULAR
    raw = pl.pallas_call(
        kernel,
        out_shape=pltpu.VMEM((864, ELEMS), F32),
        in_specs=[pl.BlockSpec(memory_space=pl.ANY)] * 5,
        out_specs=vmem,
        scratch_shapes=[
            pltpu.VMEM((3, LOCAL), F32),
            pltpu.VMEM((3, LOCAL), F32),
            pltpu.VMEM((1, LOCAL), F32),
            pltpu.VMEM((1, LOCAL), I32),
            pltpu.VMEM((1, LOCAL), I32),
            pltpu.VMEM((GRP, 8, TILE), F32),
            pltpu.VMEM((GRP, 8, TILE), F32),
            pltpu.VMEM((DEV, 4, TILE), F32),
            pltpu.VMEM((DEV, 4, TILE), F32),
            pltpu.VMEM((864, ELEMS), F32),
            pltpu.VMEM((DEV, 4, TILE), F32),
            pltpu.VMEM((DEV, 4, TILE), F32),
            pltpu.VMEM((DEV, 4, TILE), F32),
            pltpu.VMEM((8, TILE), F32),
            dma((5,)), dma, dma((2,)), dma, dma((1 + len(BOUNDS),)), regular, regular((3,)),
            regular, regular, dma, dma, dma((2,)), dma,
        ],
        compiler_params=pltpu.CompilerParams(collective_id=0, has_side_effects=True),
        name="project",
    )(
        positions,
        forces,
        volumes.reshape(1, LOCAL),
        dest_bin.reshape(1, LOCAL),
        element.reshape(1, LOCAL),
    )
    out = pl.pallas_call(
        interleave,
        out_shape=jax.ShapeDtypeStruct((864, ELEMS), F32),
        in_specs=[vmem],
        out_specs=vmem,
        name="interleave",
    )(pltpu.with_memory_space_constraint(raw, pltpu.VMEM))
    return out.reshape(4, 216, ELEMS)


def solution(mesh):
    in_specs = (
        P(None, ("grp", "dev")),
        P(None, ("grp", "dev")),
        P(("grp", "dev")),
        P(("grp", "dev"), None),
        P(("grp", "dev")),
    )
    out_specs = P(None, None, ("grp", "dev"))
    return jax.shard_map(
        per_device, mesh=mesh, in_specs=in_specs, out_specs=out_specs, check_vma=False
    )
```

```python
import functools

import jax
import jax.numpy as jnp
from jax import lax
from jax.experimental import pallas as pl
from jax.experimental.pallas import tpu as pltpu
from jax.sharding import PartitionSpec as P

MESH = pl.DeviceIdType.MESH
F32, BF16, I32 = jnp.float32, jnp.bfloat16, jnp.int32

GRP, DEV, SLOTS, LOCAL, ELEMS = 16, 32, 4, 1024, 128
TILE = 128
EARLY, LATE = 6, 10
BOUNDS = (10,)

gll_points = (
    -1.0,
    -0.765055323929465,
    -0.285231516480645,
    0.285231516480645,
    0.765055323929465,
    1.0,
)


def iota(shape, axis):
    return lax.broadcasted_iota(I32, shape, axis)


def roll(x, shift, axis):
    shift = shift % x.shape[axis]
    return x if shift == 0 else pltpu.roll(x, shift, axis)


def dot_nt(a, b):
    return lax.dot_general(a, b, (((1,), (1,)), ((), ())), preferred_element_type=F32)


def rank_in_bin(target):
    blocks = LOCAL // TILE
    row = target.astype(F32)
    parts = [row[:, b * TILE:(b + 1) * TILE] for b in range(blocks)]
    columns = [jnp.transpose(jnp.broadcast_to(part, (TILE, TILE))) for part in parts]
    earlier = iota((TILE, TILE), 0) < iota((TILE, TILE), 1)
    ranks = []
    for p in range(blocks):
        own = (columns[p] == parts[p]) & earlier
        total = jnp.where(own, 1.0, 0.0)
        for q in range(p):
            total = total + jnp.where(columns[q] == parts[p], 1.0, 0.0)
        ranks.append(jnp.sum(total, axis=0, keepdims=True))
    return jnp.concatenate(ranks, axis=1).astype(I32)


def pieces(x):
    high = x.astype(BF16).astype(F32)
    rest = x - high
    mid = rest.astype(BF16).astype(F32)
    return high, mid, rest - mid


def pack(positions, forces, volumes, target, element):
    dev = target % DEV
    code = (dev % 2) * 64 + (dev // 2) * SLOTS + rank_in_bin(target)
    row_of = iota((TILE, LOCAL), 0)
    mine = (row_of // 8) == target // DEV
    sub = iota((8, LOCAL), 0)
    parts = [positions[n:n + 1] for n in range(3)] + [element.astype(F32)]
    parts += [forces[n:n + 1] for n in range(3)] + [volumes]
    feats = parts[7]
    for n in range(7):
        feats = jnp.where(sub == n, parts[n], feats)
    left = jnp.concatenate(
        [
            jnp.where(mine, jnp.concatenate([piece] * 16, axis=0), 0.0).astype(BF16)
            for piece in pieces(feats)
        ],
        axis=0,
    )
    right = jnp.where(row_of == code, 1.0, 0.0).astype(BF16)
    prod = dot_nt(left, right)
    return prod[0:128] + prod[128:256] + prod[256:384]


def swap_halves(x):
    sub, lane = iota((8, TILE), 0), iota((8, TILE), 1)
    return jnp.where((sub // 4) == (lane // 64), x, roll(roll(x, 4, 0), 64, 1))


def to_dev_tiles(tiles):
    lane = iota((8, TILE), 1)
    for bit in range(4):
        step = 4 << bit
        low = (lane // step) % 2 == 0
        new = list(tiles)
        for v in range(16):
            if not (v >> bit) & 1:
                a, b = tiles[v], tiles[v | (1 << bit)]
                new[v] = jnp.where(low, a, roll(b, step, 1))
                new[v | (1 << bit)] = jnp.where(low, roll(a, -step, 1), b)
        tiles = new
    return [swap_halves(x) for x in tiles]


def by_row(sub, labels, parts):
    out = parts[labels[0]]
    for s in range(1, 8):
        if labels[s] != labels[s - 1]:
            out = jnp.where(sub >= s, parts[labels[s]], out)
    return out


def weigh(x):
    width = x.shape[1]
    shape = (8, width)
    sub = iota(shape, 0)
    nodes = jnp.full(shape, gll_points[5], F32)
    for n in range(5):
        nodes = jnp.where(sub == n, gll_points[n], nodes)
    w_r, w_s, w_t = [jnp.exp(-((nodes - x[d:d + 1]) ** 2) / 0.5) for d in range(3)]
    r_rows = [jnp.broadcast_to(w_r[i:i + 1], shape) for i in range(6)]
    s_cycle = (
        jnp.where(sub < 6, w_s, roll(w_s, 6, 0)),
        jnp.where(sub < 4, roll(w_s, 6, 0), roll(w_s, 4, 0)),
        jnp.where(sub < 2, roll(w_s, 4, 0), roll(w_s, 2, 0)),
    )
    faces = [
        by_row(sub, [((8 * b + s) % 36) // 6 for s in range(8)], r_rows) * s_cycle[b % 3]
        for b in range(9)
    ]
    values = [jnp.broadcast_to(x[d:d + 1], shape) for d in (7, 4, 5, 6)]
    scaled = [
        by_row(sub, [(8 * b + s) // 36 for s in range(8)], values) * faces[b % 9]
        for b in range(18)
    ]
    return scaled, w_t


def slabs(x):
    scaled, w_t = weigh(x)
    onehot = jnp.where(iota((ELEMS, x.shape[1]), 0) == x[3:4].astype(I32), 1.0, 0.0).astype(BF16)
    rows = []
    for k in range(6):
        weight = jnp.broadcast_to(w_t[k:k + 1], scaled[0].shape)
        rows += [part * weight for part in scaled]
    return dot_nt(jnp.concatenate(rows, axis=0).astype(BF16), onehot)


def face_sums(tiles):
    x = jnp.concatenate(tiles, axis=1)
    scaled, w_t = weigh(x)
    first, last = x[3:4] == 0.0, x[3:4] == ELEMS - 1.0
    weight = jnp.where(first, w_t[0:1], jnp.where(last, w_t[5:6], 0.0))
    weight = jnp.broadcast_to(weight, scaled[0].shape)
    rows = [part * weight for part in scaled]
    fill = [jnp.zeros_like(weight)] * 7
    rank, lane = iota((TILE, TILE), 0), iota((TILE, TILE), 1)
    owner = ((lane // 4) % 16) * 2 + lane // 64
    side = rank % 2
    match = owner == (rank // 4 + 1 + 30 * side) % DEV
    firsts, lasts = jnp.where(first, 1.0, 0.0), jnp.where(last, 1.0, 0.0)
    chosen = jnp.concatenate(
        [
            jnp.where(
                match & (side == 0),
                firsts[:, t:t + TILE],
                jnp.where(match & (side == 1), lasts[:, t:t + TILE], 0.0),
            )
            for t in range(0, x.shape[1], TILE)
        ],
        axis=1,
    ).astype(BF16)
    halves = [
        dot_nt(chosen, jnp.concatenate(rows[h:h + 9] + fill, axis=0).astype(BF16)) for h in (0, 9)
    ]
    return jnp.where(rank % 4 < 2, halves[0], halves[1])


CHIPS = sorted(
    [(dy, dx) for dy in range(4) for dx in range(4)],
    key=lambda m: min(m[0], 4 - m[0]) + min(m[1], 4 - m[1]),
)


def kernel(
    pos_hbm, frc_hbm, vol_hbm, bin_hbm, elem_hbm, out_ref,
    pos_ref, frc_ref, vol_ref, bin_ref, elem_ref,
    send1, recv1, send2, recv2, acc, send3, recv3, recv3x, rim,
    in_sem, send1_sem, recv1_sem, send2_sem, recv2_sem, late_sem, near_sem, row_sem, column_sem,
    slab_sem, chain_sem, send3_sem, recv3_sem, send3x_sem, recv3x_sem,
):
    g, d = lax.axis_index("grp"), lax.axis_index("dev")
    y, x, core = d // 8, (d // 2) % 4, d % 2
    late = (g + LATE) // GRP

    loads = []
    for n, (src, dst) in enumerate((
        (bin_hbm, bin_ref), (pos_hbm, pos_ref), (frc_hbm, frc_ref),
        (vol_hbm, vol_ref), (elem_hbm, elem_ref),
    )):
        load = pltpu.make_async_copy(src, dst, in_sem.at[n])
        load.start()
        loads.append(load)

    def device(dy, dx, dc):
        return (lax.rem(y + dy, 4) * 4 + lax.rem(x + dx, 4)) * 2 + lax.rem(core + dc, 2)

    def greet(sem, grp, dev):
        pl.semaphore_signal(sem, 1, device_id={"grp": grp, "dev": dev}, device_id_type=MESH)

    other = d + 1 - 2 * core
    below, above = g - EARLY, GRP - 1 - g
    row = [(0, dx, dc) for dx in (1, 3, 0) for dc in range(2) if dx or dc]
    beside, column = [(0, 1, 0), (0, 3, 0)], [(1, 0, 0), (3, 0, 0)]

    def only(condition, act):
        @pl.when(condition)
        def _():
            act()

    def greet_moves(sem, moves):
        for move in moves:
            greet(sem, g, device(*move))

    def for_late(deltas, act):
        for delta in deltas:
            inside = (late == 1) & (g + delta >= EARLY) & (g + delta < GRP)
            only(inside, functools.partial(act, g + delta))

    def greet_both(to):
        greet(barrier, to, d)
        greet(barrier, to, other)

    def in_range(delta):
        return jnp.minimum(below // delta, 1) + jnp.minimum(above // delta, 1)

    barrier = pltpu.get_barrier_semaphore()

    def greet_grp():
        for n in range(EARLY):
            only(g != n, functools.partial(greet, barrier, n, other))
        for n in range(LATE):
            greet(barrier, EARLY + n, other)

    greet_moves(barrier, row + column)
    for_late((-1, 1), greet_both)
    only(late == 0, greet_grp)

    for load in loads:
        load.wait()
    packed = pack(pos_ref[...], frc_ref[...], vol_ref[...], bin_ref[...], elem_ref[...])
    send1[...] = packed.reshape(send1.shape)

    greeted = EARLY - 1 + late * (1 + 2 * in_range(1))
    pl.semaphore_wait(barrier, len(row) + len(column) + greeted)

    def send_grp(to):
        pltpu.make_async_remote_copy(
            src_ref=send1.at[to],
            dst_ref=recv1.at[g],
            send_sem=send1_sem,
            recv_sem=recv1_sem.at[late],
            device_id={"grp": to, "dev": other},
            device_id_type=MESH,
        ).start()

    def know_slab():
        pl.semaphore_wait(row_sem, len(beside))
        greet_moves(column_sem, column)
        pl.semaphore_wait(column_sem, len(column))
        greet_moves(slab_sem, column)
        pl.semaphore_wait(slab_sem, len(column))

    def early_sends():
        for n in range(EARLY):
            only(g != n, functools.partial(send_grp, n))
        send_grp(g)
        greet_moves(row_sem, beside)
        know_slab()
        pl.semaphore_wait(late_sem, LATE)
        only(g == EARLY - 1, lambda: greet(near_sem.at[3], EARLY, d))
        only(g == 0, lambda: greet(near_sem.at[3], GRP - 1, d))
        for n in range(LATE):
            send_grp(EARLY + n)

    def late_sends():
        for n in range(EARLY):
            send_grp(n)
        for_late((-1, 1), lambda to: greet(near_sem.at[0], to, d))
        for n in range(EARLY):
            greet(late_sem, n, other)
        greet_moves(row_sem, beside)
        for_late((-1, 1), send_grp)
        send_grp(g)
        pl.semaphore_wait(near_sem.at[0], in_range(1))
        for_late((-2, 2), lambda to: greet(near_sem.at[1], to, d))
        for_late((-2, 2), send_grp)
        pl.semaphore_wait(near_sem.at[1], in_range(2))
        for_late((-4, 4), lambda to: greet(near_sem.at[2], to, d))
        for_late((-4, 4, -3, 3), send_grp)
        pl.semaphore_wait(near_sem.at[2], in_range(4))
        for_late((-8, 8, -7, 7, -6, 6, -5, 5), send_grp)
        only((g == EARLY) | (g == GRP - 1), lambda: pl.semaphore_wait(near_sem.at[3], 1))
        for_late((-9, 9), send_grp)
        know_slab()

    only(late == 0, early_sends)
    only(late == 1, late_sends)

    only(g > 0, lambda: greet(chain_sem, g - 1, other))
    only(g < GRP - 1, lambda: greet(chain_sem, g + 1, other))

    def await_grp(n, count):
        part = recv1.at[pl.ds(0, count)]
        pltpu.make_async_copy(part, part, recv1_sem.at[n]).wait()

    await_grp(0, EARLY)
    acc[0:TILE, :] = face_sums([recv1[v] for v in range(EARLY)])
    await_grp(1, LATE)
    tiles = to_dev_tiles([recv1[v] for v in range(GRP)])
    send2[...] = jnp.concatenate(tiles, axis=0).reshape(send2.shape)
    others = [
        (n, device((4 - CHIPS[n][0]) % 4, (4 - CHIPS[n][1]) % 4, dc))
        for n in range(15, -1, -1) for dc in range(2) if n or dc
    ]
    for n, peer in others:
        pltpu.make_async_remote_copy(
            src_ref=send2.at[peer],
            dst_ref=recv2.at[d],
            send_sem=send2_sem,
            recv_sem=recv2_sem.at[sum(n >= b for b in BOUNDS)],
            device_id={"grp": g, "dev": peer},
            device_id_type=MESH,
        ).start()
    recv2[d] = send2[d]

    sums = acc[0:TILE, :] + face_sums([recv1[v] for v in range(EARLY, GRP)])
    send3[...] = sums.reshape(send3.shape)
    for _, peer in others:
        pltpu.make_async_remote_copy(
            src_ref=send3.at[peer],
            dst_ref=recv3.at[d],
            send_sem=send3_sem,
            recv_sem=recv3_sem,
            device_id={"grp": g, "dev": peer},
            device_id_type=MESH,
        ).start()
    recv3[d] = send3[d]
    pl.semaphore_wait(chain_sem, jnp.minimum(g, 1) + jnp.minimum(GRP - 1 - g, 1))

    def to_slab(n, grp, dev):
        return pltpu.make_async_remote_copy(
            src_ref=send3.at[dev],
            dst_ref=recv3x.at[d],
            send_sem=send3x_sem.at[n],
            recv_sem=recv3x_sem,
            device_id={"grp": grp, "dev": dev},
            device_id_type=MESH,
        )

    @pl.when(g > 0)
    def _():
        to_slab(0, g - 1, DEV - 1).start()

    @pl.when(g < GRP - 1)
    def _():
        to_slab(1, g + 1, 0).start()

    def await_chunk(n, count):
        part = recv2.at[pl.ds(0, count)]
        pltpu.make_async_copy(part, part, recv2_sem.at[n]).wait()

    def tile(n):
        dy, dx = CHIPS[n]
        first = (lax.rem(y + dy, 4) * 4 + lax.rem(x + dx, 4)) * 2
        return swap_halves(recv2[pl.ds(first, 2)].reshape(8, TILE))

    def project(chips):
        return slabs(jnp.concatenate([tile(n) for n in chips], axis=1))

    raw = None
    for part, (low, high) in enumerate(zip((0,) + BOUNDS, BOUNDS + (16,))):
        await_chunk(part, 2 * (high - low) - (part == 0))
        if raw is not None:
            acc[...] = raw
        raw = project(range(low, high)) + (0.0 if raw is None else acc[...])
    raw0, raw5 = raw[0:144], raw[720:864]
    out_ref[144:720, :] = raw[144:720]

    rest = recv3.at[pl.ds(0, DEV - 1)]
    pltpu.make_async_copy(rest, rest, recv3_sem).wait()
    side = iota((4, TILE), 0) % 2
    keep = jnp.where(side == 0, jnp.minimum(DEV - 1 - d, 1), jnp.minimum(d, 1)).astype(F32)
    rim[...] = jnp.zeros_like(rim)
    rim[0:4, :] = keep * jnp.sum(recv3[...], axis=0)

    def add_slab(of):
        pltpu.make_async_copy(recv3x, recv3x, recv3x_sem).wait()
        rim[0:4, :] += jnp.where(side == of, jnp.sum(recv3x[...], axis=0), 0.0)

    @pl.when((d == DEV - 1) & (g < GRP - 1))
    def _():
        add_slab(0)

    @pl.when((d == 0) & (g > 0))
    def _():
        add_slab(1)

    columns = jnp.transpose(jnp.concatenate([rim[...], jnp.zeros((TILE - 8, TILE), F32)], axis=0))
    lane = iota((8, TILE), 1)
    out5, out0 = [], []
    for b in range(18):
        block0, block5 = raw0[8 * b:8 * b + 8], raw5[8 * b:8 * b + 8]
        faces, half = columns[8 * (b % 9):8 * (b % 9) + 8], 2 * (b // 9)
        after = jnp.where(lane == TILE - 1, roll(faces, TILE - 1 - half, 1), roll(block0, -1, 1))
        before = jnp.where(lane == 0, roll(faces, -1 - half, 1), roll(block5, 1, 1))
        out5.append(block5 + after)
        out0.append(block0 + before)
    out_ref[0:144, :] = jnp.concatenate(out0, axis=0)
    out_ref[720:864, :] = jnp.concatenate(out5, axis=0)

    pltpu.make_async_copy(send1, send1, send1_sem).wait()
    sent2 = send2.at[pl.ds(0, DEV - 1)]
    pltpu.make_async_copy(sent2, sent2, send2_sem).wait()
    sent3 = send3.at[pl.ds(0, DEV - 1)]
    pltpu.make_async_copy(sent3, sent3, send3_sem).wait()

    @pl.when(g > 0)
    def _():
        to_slab(0, g - 1, DEV - 1).wait_send()

    @pl.when(g < GRP - 1)
    def _():
        to_slab(1, g + 1, 0).wait_send()


def interleave(raw_ref, out_ref):
    for k in range(6):
        out_ref[pl.ds(k, 144, stride=6), :] = raw_ref[pl.ds(144 * k, 144), :]


def per_device(positions, forces, volumes, dest_bin, element):
    vmem = pl.BlockSpec(memory_space=pltpu.VMEM)
    dma, regular = pltpu.SemaphoreType.DMA, pltpu.SemaphoreType.REGULAR
    raw = pl.pallas_call(
        kernel,
        out_shape=pltpu.VMEM((864, ELEMS), F32),
        in_specs=[pl.BlockSpec(memory_space=pl.ANY)] * 5,
        out_specs=vmem,
        scratch_shapes=[
            pltpu.VMEM((3, LOCAL), F32),
            pltpu.VMEM((3, LOCAL), F32),
            pltpu.VMEM((1, LOCAL), F32),
            pltpu.VMEM((1, LOCAL), I32),
            pltpu.VMEM((1, LOCAL), I32),
            pltpu.VMEM((GRP, 8, TILE), F32),
            pltpu.VMEM((GRP, 8, TILE), F32),
            pltpu.VMEM((DEV, 4, TILE), F32),
            pltpu.VMEM((DEV, 4, TILE), F32),
            pltpu.VMEM((864, ELEMS), F32),
            pltpu.VMEM((DEV, 4, TILE), F32),
            pltpu.VMEM((DEV, 4, TILE), F32),
            pltpu.VMEM((DEV, 4, TILE), F32),
            pltpu.VMEM((8, TILE), F32),
            dma((5,)), dma, dma((2,)), dma, dma((1 + len(BOUNDS),)), regular, regular((4,)), regular, regular,
            regular, regular, dma, dma, dma((2,)), dma,
        ],
        compiler_params=pltpu.CompilerParams(collective_id=0, has_side_effects=True),
        name="project",
    )(
        positions,
        forces,
        volumes.reshape(1, LOCAL),
        dest_bin.reshape(1, LOCAL),
        element.reshape(1, LOCAL),
    )
    out = pl.pallas_call(
        interleave,
        out_shape=jax.ShapeDtypeStruct((864, ELEMS), F32),
        in_specs=[vmem],
        out_specs=vmem,
        name="interleave",
    )(pltpu.with_memory_space_constraint(raw, pltpu.VMEM))
    return out.reshape(4, 216, ELEMS)


def solution(mesh):
    in_specs = (
        P(None, ("grp", "dev")),
        P(None, ("grp", "dev")),
        P(("grp", "dev")),
        P(("grp", "dev"), None),
        P(("grp", "dev")),
    )
    out_specs = P(None, None, ("grp", "dev"))
    return jax.shard_map(
        per_device, mesh=mesh, in_specs=in_specs, out_specs=out_specs, check_vma=False
    )
```

```python
import functools

import jax
import jax.numpy as jnp
from jax import lax
from jax.experimental import pallas as pl
from jax.experimental.pallas import tpu as pltpu
from jax.sharding import PartitionSpec as P

MESH = pl.DeviceIdType.MESH
F32, BF16, I32 = jnp.float32, jnp.bfloat16, jnp.int32

GRP, DEV, SLOTS, LOCAL, ELEMS = 16, 32, 4, 1024, 128
TILE = 128
EARLY, LATE = 6, 10
BOUNDS = (10,)

gll_points = (
    -1.0,
    -0.765055323929465,
    -0.285231516480645,
    0.285231516480645,
    0.765055323929465,
    1.0,
)


def iota(shape, axis):
    return lax.broadcasted_iota(I32, shape, axis)


def roll(x, shift, axis):
    shift = shift % x.shape[axis]
    return x if shift == 0 else pltpu.roll(x, shift, axis)


def dot_nt(a, b):
    return lax.dot_general(a, b, (((1,), (1,)), ((), ())), preferred_element_type=F32)


def rank_in_bin(target):
    blocks = LOCAL // TILE
    row = target.astype(F32)
    parts = [row[:, b * TILE:(b + 1) * TILE] for b in range(blocks)]
    columns = [jnp.transpose(jnp.broadcast_to(part, (TILE, TILE))) for part in parts]
    earlier = iota((TILE, TILE), 0) < iota((TILE, TILE), 1)
    ranks = []
    for p in range(blocks):
        own = (columns[p] == parts[p]) & earlier
        total = jnp.where(own, 1.0, 0.0)
        for q in range(p):
            total = total + jnp.where(columns[q] == parts[p], 1.0, 0.0)
        ranks.append(jnp.sum(total, axis=0, keepdims=True))
    return jnp.concatenate(ranks, axis=1).astype(I32)


def pieces(x):
    high = x.astype(BF16).astype(F32)
    rest = x - high
    mid = rest.astype(BF16).astype(F32)
    return high, mid, rest - mid


def pack(positions, forces, volumes, target, element, rank):
    dev = target % DEV
    code = (dev % 2) * 64 + (dev // 2) * SLOTS + rank
    row_of = iota((TILE, LOCAL), 0)
    mine = (row_of // 8) == target // DEV
    sub = iota((8, LOCAL), 0)
    parts = [positions[n:n + 1] for n in range(3)] + [element.astype(F32)]
    parts += [forces[n:n + 1] for n in range(3)] + [volumes]
    feats = parts[7]
    for n in range(7):
        feats = jnp.where(sub == n, parts[n], feats)
    left = jnp.concatenate(
        [
            jnp.where(mine, jnp.concatenate([piece] * 16, axis=0), 0.0).astype(BF16)
            for piece in pieces(feats)
        ],
        axis=0,
    )
    right = jnp.where(row_of == code, 1.0, 0.0).astype(BF16)
    prod = dot_nt(left, right)
    return prod[0:128] + prod[128:256] + prod[256:384]


def swap_halves(x):
    sub, lane = iota((8, TILE), 0), iota((8, TILE), 1)
    return jnp.where((sub // 4) == (lane // 64), x, roll(roll(x, 4, 0), 64, 1))


def to_dev_tiles(tiles):
    lane = iota((8, TILE), 1)
    for bit in range(4):
        step = 4 << bit
        low = (lane // step) % 2 == 0
        new = list(tiles)
        for v in range(16):
            if not (v >> bit) & 1:
                a, b = tiles[v], tiles[v | (1 << bit)]
                new[v] = jnp.where(low, a, roll(b, step, 1))
                new[v | (1 << bit)] = jnp.where(low, roll(a, -step, 1), b)
        tiles = new
    return [swap_halves(x) for x in tiles]


def by_row(sub, labels, parts):
    out = parts[labels[0]]
    for s in range(1, 8):
        if labels[s] != labels[s - 1]:
            out = jnp.where(sub >= s, parts[labels[s]], out)
    return out


def weigh(x):
    width = x.shape[1]
    shape = (8, width)
    sub = iota(shape, 0)
    nodes = jnp.full(shape, gll_points[5], F32)
    for n in range(5):
        nodes = jnp.where(sub == n, gll_points[n], nodes)
    w_r, w_s, w_t = [jnp.exp(-((nodes - x[d:d + 1]) ** 2) / 0.5) for d in range(3)]
    r_rows = [jnp.broadcast_to(w_r[i:i + 1], shape) for i in range(6)]
    s_cycle = (
        jnp.where(sub < 6, w_s, roll(w_s, 6, 0)),
        jnp.where(sub < 4, roll(w_s, 6, 0), roll(w_s, 4, 0)),
        jnp.where(sub < 2, roll(w_s, 4, 0), roll(w_s, 2, 0)),
    )
    faces = [
        by_row(sub, [((8 * b + s) % 36) // 6 for s in range(8)], r_rows) * s_cycle[b % 3]
        for b in range(9)
    ]
    values = [jnp.broadcast_to(x[d:d + 1], shape) for d in (7, 4, 5, 6)]
    scaled = [
        by_row(sub, [(8 * b + s) // 36 for s in range(8)], values) * faces[b % 9]
        for b in range(18)
    ]
    return scaled, w_t


def slabs(x):
    scaled, w_t = weigh(x)
    onehot = jnp.where(iota((ELEMS, x.shape[1]), 0) == x[3:4].astype(I32), 1.0, 0.0).astype(BF16)
    rows = []
    for k in range(6):
        weight = jnp.broadcast_to(w_t[k:k + 1], scaled[0].shape)
        rows += [part * weight for part in scaled]
    return dot_nt(jnp.concatenate(rows, axis=0).astype(BF16), onehot)


def face_sums(tiles):
    x = jnp.concatenate(tiles, axis=1)
    scaled, w_t = weigh(x)
    first, last = x[3:4] == 0.0, x[3:4] == ELEMS - 1.0
    weight = jnp.where(first, w_t[0:1], jnp.where(last, w_t[5:6], 0.0))
    weight = jnp.broadcast_to(weight, scaled[0].shape)
    rows = [part * weight for part in scaled]
    fill = [jnp.zeros_like(weight)] * 7
    rank, lane = iota((TILE, TILE), 0), iota((TILE, TILE), 1)
    owner = ((lane // 4) % 16) * 2 + lane // 64
    side = rank % 2
    match = owner == (rank // 4 + 1 + 30 * side) % DEV
    firsts, lasts = jnp.where(first, 1.0, 0.0), jnp.where(last, 1.0, 0.0)
    chosen = jnp.concatenate(
        [
            jnp.where(
                match & (side == 0),
                firsts[:, t:t + TILE],
                jnp.where(match & (side == 1), lasts[:, t:t + TILE], 0.0),
            )
            for t in range(0, x.shape[1], TILE)
        ],
        axis=1,
    ).astype(BF16)
    halves = [
        dot_nt(chosen, jnp.concatenate(rows[h:h + 9] + fill, axis=0).astype(BF16)) for h in (0, 9)
    ]
    return jnp.where(rank % 4 < 2, halves[0], halves[1])


CHIPS = sorted(
    [(dy, dx) for dy in range(4) for dx in range(4)],
    key=lambda m: min(m[0], 4 - m[0]) + min(m[1], 4 - m[1]),
)


def kernel(
    pos_hbm, frc_hbm, vol_hbm, bin_hbm, elem_hbm, out_ref,
    pos_ref, frc_ref, vol_ref, bin_ref, elem_ref,
    send1, recv1, send2, recv2, acc, send3, recv3, recv3x, rim,
    in_sem, send1_sem, recv1_sem, send2_sem, recv2_sem, late_sem, near_sem, row_sem, column_sem,
    slab_sem, chain_sem, send3_sem, recv3_sem, send3x_sem, recv3x_sem,
):
    g, d = lax.axis_index("grp"), lax.axis_index("dev")
    y, x, core = d // 8, (d // 2) % 4, d % 2
    late = (g + LATE) // GRP

    loads = []
    for n, (src, dst) in enumerate((
        (bin_hbm, bin_ref), (pos_hbm, pos_ref), (frc_hbm, frc_ref),
        (vol_hbm, vol_ref), (elem_hbm, elem_ref),
    )):
        load = pltpu.make_async_copy(src, dst, in_sem.at[n])
        load.start()
        loads.append(load)

    def device(dy, dx, dc):
        return (lax.rem(y + dy, 4) * 4 + lax.rem(x + dx, 4)) * 2 + lax.rem(core + dc, 2)

    def greet(sem, grp, dev):
        pl.semaphore_signal(sem, 1, device_id={"grp": grp, "dev": dev}, device_id_type=MESH)

    other = d + 1 - 2 * core
    below, above = g - EARLY, GRP - 1 - g
    row = [(0, dx, dc) for dx in (1, 3, 0) for dc in range(2) if dx or dc]
    beside, column = [(0, 1, 0), (0, 3, 0)], [(1, 0, 0), (3, 0, 0)]

    def only(condition, act):
        @pl.when(condition)
        def _():
            act()

    def greet_moves(sem, moves):
        for move in moves:
            greet(sem, g, device(*move))

    def for_late(deltas, act):
        for delta in deltas:
            inside = (late == 1) & (g + delta >= EARLY) & (g + delta < GRP)
            only(inside, functools.partial(act, g + delta))

    def greet_both(to):
        greet(barrier, to, d)
        greet(barrier, to, other)

    def in_range(delta):
        return jnp.minimum(below // delta, 1) + jnp.minimum(above // delta, 1)

    barrier = pltpu.get_barrier_semaphore()

    def greet_grp():
        for n in range(EARLY):
            only(g != n, functools.partial(greet, barrier, n, other))
        for n in range(LATE):
            greet(barrier, EARLY + n, other)

    greet_moves(barrier, row + column)
    for_late((-1, 1), greet_both)
    only(late == 0, greet_grp)

    loads[0].wait()
    target = bin_ref[...]
    rank = rank_in_bin(target)
    for load in loads[1:]:
        load.wait()
    packed = pack(pos_ref[...], frc_ref[...], vol_ref[...], target, elem_ref[...], rank)
    send1[...] = packed.reshape(send1.shape)

    greeted = EARLY - 1 + late * (1 + 2 * in_range(1))
    pl.semaphore_wait(barrier, len(row) + len(column) + greeted)

    def send_grp(to):
        pltpu.make_async_remote_copy(
            src_ref=send1.at[to],
            dst_ref=recv1.at[g],
            send_sem=send1_sem,
            recv_sem=recv1_sem.at[late],
            device_id={"grp": to, "dev": other},
            device_id_type=MESH,
        ).start()

    def know_slab():
        pl.semaphore_wait(row_sem, len(beside))
        greet_moves(column_sem, column)
        pl.semaphore_wait(column_sem, len(column))
        greet_moves(slab_sem, column)
        pl.semaphore_wait(slab_sem, len(column))

    def early_sends():
        for n in range(EARLY):
            only(g != n, functools.partial(send_grp, n))
        send_grp(g)
        greet_moves(row_sem, beside)
        know_slab()
        pl.semaphore_wait(late_sem, LATE)
        only(g == EARLY - 1, lambda: greet(near_sem.at[3], EARLY, d))
        only(g == 0, lambda: greet(near_sem.at[3], GRP - 1, d))
        for n in range(LATE):
            send_grp(EARLY + n)

    def late_sends():
        for_late((-1, 1), lambda to: greet(near_sem.at[0], to, d))
        for n in range(EARLY):
            send_grp(n)
        for n in range(EARLY):
            greet(late_sem, n, other)
        greet_moves(row_sem, beside)
        for_late((-1, 1), send_grp)
        send_grp(g)
        pl.semaphore_wait(near_sem.at[0], in_range(1))
        for_late((-2, 2), lambda to: greet(near_sem.at[1], to, d))
        for_late((-2, 2), send_grp)
        pl.semaphore_wait(near_sem.at[1], in_range(2))
        for_late((-4, 4), lambda to: greet(near_sem.at[2], to, d))
        for_late((-4, 4, -3, 3), send_grp)
        pl.semaphore_wait(near_sem.at[2], in_range(4))
        for_late((-8, 8, -7, 7, -6, 6, -5, 5), send_grp)
        only((g == EARLY) | (g == GRP - 1), lambda: pl.semaphore_wait(near_sem.at[3], 1))
        for_late((-9, 9), send_grp)
        know_slab()

    only(late == 0, early_sends)
    only(late == 1, late_sends)

    only(g > 0, lambda: greet(chain_sem, g - 1, other))
    only(g < GRP - 1, lambda: greet(chain_sem, g + 1, other))

    def await_grp(n, count):
        part = recv1.at[pl.ds(0, count)]
        pltpu.make_async_copy(part, part, recv1_sem.at[n]).wait()

    await_grp(0, EARLY)
    acc[0:TILE, :] = face_sums([recv1[v] for v in range(EARLY)])
    await_grp(1, LATE)
    tiles = to_dev_tiles([recv1[v] for v in range(GRP)])
    send2[...] = jnp.concatenate(tiles, axis=0).reshape(send2.shape)
    others = [
        (n, device((4 - CHIPS[n][0]) % 4, (4 - CHIPS[n][1]) % 4, dc))
        for n in range(15, -1, -1) for dc in range(2) if n or dc
    ]
    for n, peer in others:
        pltpu.make_async_remote_copy(
            src_ref=send2.at[peer],
            dst_ref=recv2.at[d],
            send_sem=send2_sem,
            recv_sem=recv2_sem.at[sum(n >= b for b in BOUNDS)],
            device_id={"grp": g, "dev": peer},
            device_id_type=MESH,
        ).start()
    recv2[d] = send2[d]

    sums = acc[0:TILE, :] + face_sums([recv1[v] for v in range(EARLY, GRP)])
    send3[...] = sums.reshape(send3.shape)
    for _, peer in others:
        pltpu.make_async_remote_copy(
            src_ref=send3.at[peer],
            dst_ref=recv3.at[d],
            send_sem=send3_sem,
            recv_sem=recv3_sem,
            device_id={"grp": g, "dev": peer},
            device_id_type=MESH,
        ).start()
    recv3[d] = send3[d]
    pl.semaphore_wait(chain_sem, jnp.minimum(g, 1) + jnp.minimum(GRP - 1 - g, 1))

    def to_slab(n, grp, dev):
        return pltpu.make_async_remote_copy(
            src_ref=send3.at[dev],
            dst_ref=recv3x.at[d],
            send_sem=send3x_sem.at[n],
            recv_sem=recv3x_sem,
            device_id={"grp": grp, "dev": dev},
            device_id_type=MESH,
        )

    @pl.when(g > 0)
    def _():
        to_slab(0, g - 1, DEV - 1).start()

    @pl.when(g < GRP - 1)
    def _():
        to_slab(1, g + 1, 0).start()

    def await_chunk(n, count):
        part = recv2.at[pl.ds(0, count)]
        pltpu.make_async_copy(part, part, recv2_sem.at[n]).wait()

    def tile(n):
        dy, dx = CHIPS[n]
        first = (lax.rem(y + dy, 4) * 4 + lax.rem(x + dx, 4)) * 2
        return swap_halves(recv2[pl.ds(first, 2)].reshape(8, TILE))

    def project(chips):
        return slabs(jnp.concatenate([tile(n) for n in chips], axis=1))

    raw = None
    for part, (low, high) in enumerate(zip((0,) + BOUNDS, BOUNDS + (16,))):
        await_chunk(part, 2 * (high - low) - (part == 0))
        if raw is not None:
            acc[...] = raw
        raw = project(range(low, high)) + (0.0 if raw is None else acc[...])
    raw0, raw5 = raw[0:144], raw[720:864]
    out_ref[144:720, :] = raw[144:720]

    rest = recv3.at[pl.ds(0, DEV - 1)]
    pltpu.make_async_copy(rest, rest, recv3_sem).wait()
    side = iota((4, TILE), 0) % 2
    keep = jnp.where(side == 0, jnp.minimum(DEV - 1 - d, 1), jnp.minimum(d, 1)).astype(F32)
    rim[...] = jnp.zeros_like(rim)
    rim[0:4, :] = keep * jnp.sum(recv3[...], axis=0)

    def add_slab(of):
        pltpu.make_async_copy(recv3x, recv3x, recv3x_sem).wait()
        rim[0:4, :] += jnp.where(side == of, jnp.sum(recv3x[...], axis=0), 0.0)

    @pl.when((d == DEV - 1) & (g < GRP - 1))
    def _():
        add_slab(0)

    @pl.when((d == 0) & (g > 0))
    def _():
        add_slab(1)

    columns = jnp.transpose(jnp.concatenate([rim[...], jnp.zeros((TILE - 8, TILE), F32)], axis=0))
    lane = iota((8, TILE), 1)
    out5, out0 = [], []
    for b in range(18):
        block0, block5 = raw0[8 * b:8 * b + 8], raw5[8 * b:8 * b + 8]
        faces, half = columns[8 * (b % 9):8 * (b % 9) + 8], 2 * (b // 9)
        after = jnp.where(lane == TILE - 1, roll(faces, TILE - 1 - half, 1), roll(block0, -1, 1))
        before = jnp.where(lane == 0, roll(faces, -1 - half, 1), roll(block5, 1, 1))
        out5.append(block5 + after)
        out0.append(block0 + before)
    out_ref[0:144, :] = jnp.concatenate(out0, axis=0)
    out_ref[720:864, :] = jnp.concatenate(out5, axis=0)

    pltpu.make_async_copy(send1, send1, send1_sem).wait()
    sent2 = send2.at[pl.ds(0, DEV - 1)]
    pltpu.make_async_copy(sent2, sent2, send2_sem).wait()
    sent3 = send3.at[pl.ds(0, DEV - 1)]
    pltpu.make_async_copy(sent3, sent3, send3_sem).wait()

    @pl.when(g > 0)
    def _():
        to_slab(0, g - 1, DEV - 1).wait_send()

    @pl.when(g < GRP - 1)
    def _():
        to_slab(1, g + 1, 0).wait_send()


def interleave(raw_ref, out_ref):
    for k in range(6):
        out_ref[pl.ds(k, 144, stride=6), :] = raw_ref[pl.ds(144 * k, 144), :]


def per_device(positions, forces, volumes, dest_bin, element):
    vmem = pl.BlockSpec(memory_space=pltpu.VMEM)
    dma, regular = pltpu.SemaphoreType.DMA, pltpu.SemaphoreType.REGULAR
    raw = pl.pallas_call(
        kernel,
        out_shape=pltpu.VMEM((864, ELEMS), F32),
        in_specs=[pl.BlockSpec(memory_space=pl.ANY)] * 5,
        out_specs=vmem,
        scratch_shapes=[
            pltpu.VMEM((3, LOCAL), F32),
            pltpu.VMEM((3, LOCAL), F32),
            pltpu.VMEM((1, LOCAL), F32),
            pltpu.VMEM((1, LOCAL), I32),
            pltpu.VMEM((1, LOCAL), I32),
            pltpu.VMEM((GRP, 8, TILE), F32),
            pltpu.VMEM((GRP, 8, TILE), F32),
            pltpu.VMEM((DEV, 4, TILE), F32),
            pltpu.VMEM((DEV, 4, TILE), F32),
            pltpu.VMEM((864, ELEMS), F32),
            pltpu.VMEM((DEV, 4, TILE), F32),
            pltpu.VMEM((DEV, 4, TILE), F32),
            pltpu.VMEM((DEV, 4, TILE), F32),
            pltpu.VMEM((8, TILE), F32),
            dma((5,)), dma, dma((2,)), dma, dma((1 + len(BOUNDS),)), regular, regular((4,)), regular, regular,
            regular, regular, dma, dma, dma((2,)), dma,
        ],
        compiler_params=pltpu.CompilerParams(collective_id=0, has_side_effects=True),
        name="project",
    )(
        positions,
        forces,
        volumes.reshape(1, LOCAL),
        dest_bin.reshape(1, LOCAL),
        element.reshape(1, LOCAL),
    )
    out = pl.pallas_call(
        interleave,
        out_shape=jax.ShapeDtypeStruct((864, ELEMS), F32),
        in_specs=[vmem],
        out_specs=vmem,
        name="interleave",
    )(pltpu.with_memory_space_constraint(raw, pltpu.VMEM))
    return out.reshape(4, 216, ELEMS)


def solution(mesh):
    in_specs = (
        P(None, ("grp", "dev")),
        P(None, ("grp", "dev")),
        P(("grp", "dev")),
        P(("grp", "dev"), None),
        P(("grp", "dev")),
    )
    out_specs = P(None, None, ("grp", "dev"))
    return jax.shard_map(
        per_device, mesh=mesh, in_specs=in_specs, out_specs=out_specs, check_vma=False
    )
```
